256 devices in a mesh: dp: 64 (over z, y_lo, x), tensor: 4 (over y_hi, core).
Axes of the slice: x: 4, y: 4 (y_hi: 2, y_lo: 2; y = y_hi * 2 + y_lo), z: 8, core: 2. Of those that a mesh axis runs over, the one named last changes fastest.
Arguments:
- queries: bfloat16 [32768, 2048], P('dp', 'tensor'), may hold values from -2.5 to 2.5
- keys: bfloat16 [32768, 2048], P('dp', 'tensor'), may hold values from -2.5 to 2.5
- values: bfloat16 [32768, 2048], P('dp', 'tensor'), may hold values from -6 to 6
- attended: bfloat16 [32768, 2048], P('dp', 'tensor'), may hold values from -6 to 6
- upstream: bfloat16 [32768, 4096], P(('dp', 'tensor')), may hold values from -24 to 24
- out_weight: bfloat16 [2048, 4096], P('tensor', 'dp'), may hold values from -0.125 to 0.125
- bias_table: float32 [32, 32], P(None, 'tensor'), may hold values from -4 to 4
- buckets: int32 [511], replicated, may hold values from 0 to 31
- segments: int32 [32768], P('dp'), may hold values from 0 to 2, as said below
Outputs:
- query_grad: bfloat16 [32768, 2048], P('dp', 'tensor')
- key_grad: bfloat16 [32768, 2048], P('dp', 'tensor')
- value_grad: bfloat16 [32768, 2048], P('dp', 'tensor')
- weight_grad: float32 [4096, 2048], P('dp', 'tensor')
- table_grad: float32 [32, 32], P(None, 'tensor')
The draws below stay inside these ranges and needn't reach their ends.
Inputs may be any that keep to these rules, and one draw needn't show every extreme that they name: `segments`: within each group of 512 rows, ids start at 0 and rise by one at each passage boundary; every passage has at most 256 tokens and the group holds one of exactly 256.
All inputs are finite; a program needn't handle non-finite values.
Results may differ from the reference program's by a relative error of at most 0.0076.
Values may be sent and summed in bfloat16 or wider, within the bound.
A program may use at most 64 MiB of HBM per device.

```python
import jax
import jax.numpy as jnp
from jax import lax

D = 4096
H = 32
HDIM = 64
NB = 32
PLEN = 256
ROWS = 512
TOKENS = 32768
HD = 2048


def paired_draw(key):
    base = jax.random.fold_in(key, 11)
    key_q, key_k = jax.random.split(base, 2)
    width = H * HDIM
    query_part = jnp.clip(0.2 * jax.random.normal(key_q, (TOKENS, width), jnp.float32), -1.2, 1.2)
    key_part = jnp.clip(0.2 * jax.random.normal(key_k, (TOKENS, width), jnp.float32), -1.2, 1.2)
    return (query_part, key_part)


def draw_queries(key, part):
    return paired_draw(key)[0].astype(jnp.bfloat16)


def draw_keys(key, part):
    return paired_draw(key)[1].astype(jnp.bfloat16)


def draw_segments(key, part):
    groups = TOKENS // ROWS
    shifts = jax.random.randint(jax.random.fold_in(key, 23), (groups,), 1, PLEN)
    local = jnp.arange(ROWS, dtype=jnp.int32)
    ids = (local[None, :] + shifts[:, None]) // PLEN
    return ids.reshape(TOKENS).astype(jnp.int32)


def touch_ends(drawn, own_key, smallest, high):
    longest = drawn.shape.index(max(drawn.shape))
    spots = []
    for shift in (0, 1):
        where = [jax.random.randint(jax.random.fold_in(own_key, axis), (), 0, length) for axis, length in enumerate(drawn.shape)]
        where[longest] = (where[longest] + shift) % drawn.shape[longest]
        spots.append(tuple(where))
    return drawn.at[spots[0]].set(smallest).at[spots[1]].set(high)


def raised(array, stream_key, source, target, blocks, factor):
    def block_of(axis_at):
        return (jnp.arange(array.shape[axis_at]) // (array.shape[axis_at] // blocks)).reshape((-1,) + (1,) * (array.ndim - 1 - axis_at))

    one_side = jax.random.permutation(stream_key, blocks)[block_of(target)]
    second = (block_of(target) + blocks // 2) % blocks
    return jnp.where((block_of(source) == one_side) | (block_of(source) == second), factor * array, array)


def levels(rng, shape, shards, smallest, largest):
    level = 1.0
    for dim, shards_of in shards:
        heights = jax.random.uniform(jax.random.fold_in(jax.random.fold_in(rng, 6), dim), (shards_of,), jnp.float32, smallest / len(shards), largest / len(shards))
        level = level * jnp.repeat(jnp.exp(heights), shape[dim] // shards_of).reshape((-1,) + (1,) * (len(shape) - 1 - dim))
    return level


def scatter_about(stream_key, extent, deviation, limit, cuts=(), held_as=jnp.bfloat16):
    values = jax.random.normal(stream_key, extent, jnp.float32) * deviation
    if len(cuts) > 0:
        values = levels(stream_key, extent, cuts, -0.22, 0.18) * values
    return jnp.clip(values, min=-limit, max=limit).astype(held_as)


def bell_draw_with(stream_key, shape, spread, reach, pieces, heavy, kind=jnp.bfloat16):
    array = spread * jax.random.normal(stream_key, shape, jnp.float32)
    if pieces:
        array = array * levels(stream_key, shape, pieces, -0.22, 0.18)
    return jnp.clip(raised(array, jax.random.fold_in(stream_key, 3), *heavy), -reach, reach).astype(kind)


def setup_inputs(seed: int = 0) -> dict:
    arg_keys = jax.random.split(jax.random.key(seed), 10)
    return {
        "queries": draw_queries(jax.random.fold_in(arg_keys[9], 71), 0),
        "keys": draw_keys(jax.random.fold_in(arg_keys[9], 71), 0),
        "values": scatter_about(arg_keys[2], (TOKENS, HD), 1.0, 6.0, ((0, 64), (1, 4))),
        "attended": scatter_about(arg_keys[3], (TOKENS, HD), 1.0, 6.0, ((0, 64), (1, 4))),
        "upstream": bell_draw_with(arg_keys[4], (TOKENS, D), 1.0, 24.0, ((0, 256),), (0, 1, 256, 6.0)),
        "out_weight": scatter_about(arg_keys[5], (HD, D), HD ** -0.5, 0.125, ((0, 4), (1, 64))),
        "bias_table": scatter_about(arg_keys[6], (NB, H), 1.0, 4.0, ((1, 4),), jnp.float32),
        "buckets": touch_ends(jax.random.randint(arg_keys[7], (2 * PLEN - 1,), 0, NB), jax.random.fold_in(arg_keys[7], 1), 0, NB - 1).astype(jnp.int32),
        "segments": draw_segments(jax.random.fold_in(arg_keys[9], 71), 0),
    }


def head_backward(items, index, same, offsets):
    q_head, k_head, v_head, g_head, bias_col = items
    scores = lax.dot_general(q_head, k_head, (((1,), (1,)), ((), ())), preferred_element_type=jnp.float32)
    scores = scores + bias_col[index]
    scores = jnp.where(same, scores, -jnp.inf)
    peak = jnp.max(scores, axis=1, keepdims=True)
    expd = jnp.exp(scores - peak)
    probs = expd / jnp.sum(expd, axis=1, keepdims=True)
    probs_b = probs.astype(jnp.bfloat16)
    dprobs = lax.dot_general(g_head, v_head, (((1,), (1,)), ((), ())), preferred_element_type=jnp.float32)
    delta = jnp.sum(probs * dprobs, axis=1, keepdims=True)
    dscores = probs * (dprobs - delta)
    ds_b = dscores.astype(jnp.bfloat16)
    q_grad = jnp.dot(ds_b, k_head, preferred_element_type=jnp.float32).astype(jnp.bfloat16)
    k_grad = lax.dot_general(ds_b, q_head, (((0,), (0,)), ((), ())), preferred_element_type=jnp.float32).astype(jnp.bfloat16)
    v_grad = lax.dot_general(probs_b, g_head, (((0,), (0,)), ((), ())), preferred_element_type=jnp.float32).astype(jnp.bfloat16)
    off_grad = jax.ops.segment_sum(dscores.reshape(-1), index.reshape(-1), num_segments=offsets)
    return q_grad, k_grad, v_grad, off_grad


def reference(queries, keys, values, attended, upstream, out_weight, bias_table, buckets, segments):
    grad_ctx = lax.dot_general(upstream, out_weight, (((1,), (1,)), ((), ())), preferred_element_type=jnp.float32).astype(jnp.bfloat16)
    weight_grad = lax.dot_general(upstream, attended, (((0,), (0,)), ((), ())), preferred_element_type=jnp.float32)
    offsets = 2 * PLEN - 1
    onehot = (buckets[:, None] == jnp.arange(NB, dtype=jnp.int32)[None, :]).astype(jnp.float32)
    bias_off = jnp.dot(onehot, bias_table, precision=lax.Precision.HIGHEST)
    position = jnp.arange(ROWS, dtype=jnp.int32)
    index = jnp.clip(position[:, None] - position[None, :] + PLEN - 1, 0, offsets - 1).astype(jnp.int32)
    groups = TOKENS // ROWS

    def split(block):
        return block.reshape(ROWS, H, HDIM).transpose(1, 0, 2)

    def join(stacked):
        return stacked.transpose(1, 0, 2).reshape(ROWS, H * HDIM)

    def per_group(items):
        q_all, k_all, v_all, g_all, seg = items
        same = seg[:, None] == seg[None, :]

        def one_head(head_items):
            return head_backward(head_items, index, same, offsets)

        q_grad, k_grad, v_grad, off_grad = lax.map(one_head, (split(q_all), split(k_all), split(v_all), split(g_all), bias_off.T))
        return join(q_grad), join(k_grad), join(v_grad), off_grad

    stacked = (queries.reshape(groups, ROWS, H * HDIM), keys.reshape(groups, ROWS, H * HDIM),
               values.reshape(groups, ROWS, H * HDIM), grad_ctx.reshape(groups, ROWS, H * HDIM),
               segments.reshape(groups, ROWS))
    q_grad, k_grad, v_grad, off_grad = lax.map(per_group, stacked)
    table_grad = jnp.dot(onehot.T, jnp.sum(off_grad, axis=0).T, precision=lax.Precision.HIGHEST)
    return (q_grad.reshape(TOKENS, H * HDIM), k_grad.reshape(TOKENS, H * HDIM),
            v_grad.reshape(TOKENS, H * HDIM), weight_grad, table_grad)
```

```python
import functools

import jax
import jax.numpy as jnp
from jax import lax
from jax.experimental import pallas as pl
from jax.experimental.pallas import tpu as pltpu
from jax.sharding import PartitionSpec as P

MESH = pl.DeviceIdType.MESH
F32 = jnp.float32
BF16 = jnp.bfloat16
ROWS = 512
FEAT = 512
HALF = 256
D = 4096
HEADS = 8
WIDE = 768
BLOCK = 128
FAR = -4096.0
N_SEM = 96


def nt(a, b):
    return lax.dot_general(a, b, (((1,), (1,)), ((), ())), preferred_element_type=F32)


def nn(a, b):
    return jnp.dot(a, b, preferred_element_type=F32)


class Wire:
    def __init__(self, send_sem, recv_sem):
        self.send_sem, self.recv_sem = send_sem, recv_sem
        self.made = []

    def send(self, src, dst, device):
        at = len(self.made)
        copy = pltpu.make_async_remote_copy(
            src_ref=src,
            dst_ref=dst,
            send_sem=self.send_sem.at[at],
            recv_sem=self.recv_sem.at[at],
            device_id=device,
            device_id_type=MESH,
        )
        copy.start()
        self.made.append(copy)
        return copy

    def finish(self):
        for copy in self.made:
            copy.wait_send()


def kernel(
    q_hbm, k_hbm, v_hbm, att_hbm, up_hbm, wt_hbm, table_ref, bucket_ref, seg_ref,
    dq_ref, dk_ref, dv_ref, wg_ref, tg_ref,
    q_ref, k_ref, v_ref, att_ref, g_ref, ctx_ref, wa_ref, wb_ref, fp_ref, fm_ref,
    ta_ref, tb_ref, rap_ref, ram_ref, sa_ref, saf_ref, rax_ref, ray_ref, say_ref,
    rbp_ref, rbm_ref, sby_ref, sbf_ref, rby_ref, sbz_ref, rbz_ref,
    e_ref, r_ref, dp_ref, pb_ref, dsb_ref, toe_ref, bext_ref, oh_ref, gb_ref, g8_ref,
    qaug_ref, kaug_ref, dqt_ref, dkp_ref, dvp_ref,
    tz_ref, rtz_ref, tx_ref, rtx_ref, ty_ref, rty_ref,
    local_sem, send_sem, recv_sem,
):
    me, tensor = lax.axis_index("dp"), lax.axis_index("tensor")
    x, yl, z = lax.rem(me, 4), lax.rem(lax.div(me, 4), 2), lax.div(me, 8)
    core, yh = lax.rem(tensor, 2), lax.div(tensor, 2)
    y = yh * 2 + yl

    def place(z_at, yl_at, x_at, yh_at, core_at):
        return {"dp": z_at * 8 + yl_at * 4 + x_at, "tensor": yh_at * 2 + core_at}

    def xs(k):
        return lax.rem(x + k, 4)

    def zs(k):
        return lax.rem(z + k, 8)

    def at_x(k):
        return place(z, yl, xs(k), yh, core)

    def at_z(k):
        return place(zs(k), yl, x, yh, core)

    def at_y(k):
        there = lax.rem(y + k, 4)
        return place(z, lax.rem(there, 2), x, lax.div(there, 2), core)

    pair = place(z, 1 - yl, x, yh, core)
    mate = place(z, yl, x, yh, 1 - core)

    loads = []
    for at, (src, dst) in enumerate(
        [
            (q_hbm, q_ref),
            (k_hbm, k_ref),
            (v_hbm, v_ref),
            (att_hbm, att_ref),
            (up_hbm, g_ref.at[pl.ds(pl.multiple_of(tensor * 128, 128), 128), :]),
            (wt_hbm.at[:, pl.ds(0, HALF)], wa_ref.at[z, yl, x]),
            (wt_hbm.at[:, pl.ds(HALF, HALF)], wb_ref.at[z, yl, x]),
        ]
    ):
        copy = pltpu.make_async_copy(src, dst, local_sem.at[at])
        copy.start()
        loads.append(copy)

    barrier = pltpu.get_barrier_semaphore()
    greeted = [at_z(k) for k in range(1, 8)] + [at_x(k) for k in range(1, 4)] + [at_y(1), at_y(3), mate]
    for device in greeted:
        pl.semaphore_signal(barrier, inc=1, device_id=device, device_id_type=MESH)
    pl.semaphore_wait(barrier, len(greeted))

    wire = Wire(send_sem, recv_sem)

    y_pair = wire.send(wt_hbm.at[:, pl.ds(0, HALF)], wa_ref.at[z, yl, x], pair)
    b_z = [
        wire.send(wt_hbm.at[:, pl.ds(HALF, HALF)], wb_ref.at[z, yl, x], at_z(k)) for k in range(1, 8)
    ]
    own_rows = pl.multiple_of(tensor * 128, 128)
    up_fp, up_fm = [], []
    for c in range(2):
        up_fp.append(wire.send(up_hbm.at[pl.ds(c * 32, 32), :], fp_ref.at[c], at_y(1)))
        up_fm.append(wire.send(up_hbm.at[pl.ds(64 + c * 32, 32), :], fm_ref.at[c], at_y(3)))
    to_mate = [wire.send(up_hbm, g_ref.at[pl.ds(own_rows, 128), :], mate)]
    for copy in loads:
        copy.wait()

    before = lax.div(lax.rem(y + 3, 4), 2) * 2 + core
    after = lax.div(lax.rem(y + 1, 4), 2) * 2 + core
    across = (1 - yh) * 2 + core
    got = {}

    def gather_a2():
        y_pair.wait_recv()
        got["a_x"] = [wire.send(wa_ref.at[z, :, x], wa_ref.at[z, :, x], at_x(k)) for k in (1, 3, 2)]

    def a_hop(step, way, part):
        chunk = wa_ref.at[zs(8 - (step - 1) if way == 1 else step - 1), part]
        return wire.send(chunk, chunk, at_z(1 if way == 1 else 7))

    def gather_a3():
        for copy in got["a_x"]:
            copy.wait_recv()
        for part in range(2):
            for way in (1, -1):
                got["a_z", 1, way, part] = a_hop(1, way, part)

    def gather_a_step(step):
        for part in range(2):
            for way in (1, -1):
                got["a_z", step, way, part].wait_recv()
                if step < 3 or (part == 0) == (way == 1):
                    got["a_z", step + 1, way, part] = a_hop(step + 1, way, part)

    def gather_a_end():
        got["a_z", 4, 1, 0].wait_recv()
        got["a_z", 4, -1, 1].wait_recv()

    def gather_b2():
        for copy in b_z:
            copy.wait_recv()
        got["b_y"] = wire.send(wb_ref.at[:, yl, x], wb_ref.at[:, yl, x], pair)

    def gather_b3():
        got["b_y"].wait_recv()
        for part in range(2):
            chunk = wb_ref.at[pl.ds(part * 4, 4), :, x]
            for way in (1, 3):
                got["b_x", 1, way, part] = wire.send(chunk, chunk, at_x(way))

    def gather_b4(part):
        for way in (1, 3):
            got["b_x", 1, way, part].wait_recv()
        way = 1 if part == 0 else 3
        chunk = wb_ref.at[pl.ds(part * 4, 4), :, xs(3 if part == 0 else 1)]
        got["b_x", 2, part] = wire.send(chunk, chunk, at_x(way))

    def gather_b_end():
        for part in range(2):
            got["b_x", 2, part].wait_recv()

    def rows_of(owner, first, count):
        return g_ref.at[pl.ds(pl.multiple_of(owner * 128 + first, 32), count), :]

    def up_hand_on(c):
        up_fp[c].wait_recv()
        got["u", 0, c] = wire.send(fp_ref.at[c], rows_of(before, c * 32, 32), at_y(1))
        up_fm[c].wait_recv()
        got["u", 1, c] = wire.send(fm_ref.at[c], rows_of(after, 64 + c * 32, 32), at_y(3))

    def up_share(c):
        for side in range(2):
            got["u", side, c].wait_recv()
            block = rows_of(across, side * 64 + c * 32, 32)
            to_mate.append(wire.send(block, block, mate))

    def up_end():
        for copy in to_mate:
            copy.wait_recv()

    def prepare():
        lane = lax.broadcasted_iota(jnp.int32, (ROWS, BLOCK), 1)
        spot = jnp.where(lane < 64, lane, lane - 64)
        seg = jnp.broadcast_to(seg_ref[...].astype(F32), (BLOCK, ROWS)).T
        same = seg == spot.astype(F32)
        qaug_ref[...] = jnp.where(same, 1.0, 0.0).astype(BF16)
        kaug_ref[...] = jnp.where((spot < 3) & jnp.logical_not(same), FAR, 0.0).astype(BF16)
        oh_ref[...] = jnp.where(
            lax.broadcasted_iota(jnp.int32, (32, WIDE), 0) == bucket_ref[...], 1.0, 0.0
        )
        bext_ref[...] = jnp.dot(
            table_ref[...], oh_ref[...], precision=lax.Precision.HIGHEST, preferred_element_type=F32
        )
        pb_ref[...] = jnp.zeros_like(pb_ref)
        dsb_ref[...] = jnp.zeros_like(dsb_ref)

    def columns(p):
        return pl.ds(pl.multiple_of(p * BLOCK, BLOCK), BLOCK)

    def own_lanes(odd):
        lane = lax.broadcasted_iota(jnp.int32, (ROWS, BLOCK), 1)
        return (lane >= 64) if odd else (lane < 64)

    def softmax_pair(p):
        qp, kp = q_ref[:, columns(p)], k_ref[:, columns(p)]
        for odd in range(2):
            h = 2 * p + odd
            own = own_lanes(odd)
            q_h = jnp.where(own, qp, qaug_ref[...])
            k_h = jnp.where(own, kp, kaug_ref[...])
            bias = bext_ref[pl.ds(h, 1), :]
            for d in range(5):
                strip = jnp.broadcast_to(bias[:, d * BLOCK : (d + 2) * BLOCK], (BLOCK, 2 * BLOCK))
                toe_ref[d] = pltpu.roll(strip, 0, 1, stride=1, stride_axis=0)[:, BLOCK:]
            for i2 in range(2):
                peak = [None, None]
                for j in range(4):
                    s2 = nt(k_h[j * BLOCK : (j + 1) * BLOCK], q_h[i2 * 256 : (i2 + 1) * 256])
                    for sub in range(2):
                        i = 2 * i2 + sub
                        if abs(i - j) <= 2:
                            s = s2[:, sub * BLOCK : (sub + 1) * BLOCK] + toe_ref[i - j + 2]
                            e_ref[h, j * BLOCK : (j + 1) * BLOCK, i * BLOCK : (i + 1) * BLOCK] = s
                            top = jnp.max(s.reshape(16, 8, BLOCK), axis=0)
                            peak[sub] = top if peak[sub] is None else jnp.maximum(peak[sub], top)
                for sub in range(2):
                    i = 2 * i2 + sub
                    top = jnp.max(peak[sub], axis=0, keepdims=True)
                    total = None
                    for j in range(4):
                        if abs(i - j) <= 2:
                            at = (h, slice(j * BLOCK, (j + 1) * BLOCK), slice(i * BLOCK, (i + 1) * BLOCK))
                            e = jnp.exp(e_ref[at] - top)
                            e_ref[at] = e
                            part = jnp.sum(e.reshape(16, 8, BLOCK), axis=0)
                            total = part if total is None else total + part
                    r_ref[pl.ds(h, 1), i * BLOCK : (i + 1) * BLOCK] = 1.0 / jnp.sum(
                        total, axis=0, keepdims=True
                    )

    def context(which, m):
        w = (wa_ref if which == 0 else wb_ref)[...].reshape(D, HALF)
        rows = slice(m * 256, (m + 1) * 256)
        ctx_ref[rows, which * HALF : (which + 1) * HALF] = nn(g_ref[rows, :], w).astype(BF16)

    def backward_pair(p):
        qp, kp = q_ref[:, columns(p)], k_ref[:, columns(p)]
        vp, gp = v_ref[:, columns(p)], ctx_ref[:, columns(p)]
        kpt = kp.T
        for odd in range(2):
            h = 2 * p + odd
            own = own_lanes(odd)
            g_h = jnp.where(own, gp, jnp.zeros_like(gp))
            delta = []
            for i2 in range(2):
                sums = [None, None]
                for j in range(4):
                    d2 = nt(vp[j * BLOCK : (j + 1) * BLOCK], g_h[i2 * 256 : (i2 + 1) * 256])
                    for sub in range(2):
                        i = 2 * i2 + sub
                        if abs(i - j) <= 2:
                            js, cs = slice(j * BLOCK, (j + 1) * BLOCK), slice(i * BLOCK, (i + 1) * BLOCK)
                            d1 = d2[:, sub * BLOCK : (sub + 1) * BLOCK]
                            dp_ref[js, cs] = d1
                            part = jnp.sum((e_ref[h, js, cs] * d1).reshape(16, 8, BLOCK), axis=0)
                            sums[sub] = part if sums[sub] is None else sums[sub] + part
                for sub in range(2):
                    i = 2 * i2 + sub
                    recip = r_ref[pl.ds(h, 1), i * BLOCK : (i + 1) * BLOCK]
                    delta.append(recip * jnp.sum(sums[sub], axis=0, keepdims=True))
            g8_ref[...] = jnp.zeros_like(g8_ref)
            for d in range(-2, 3):
                diag = None
                for j in range(4):
                    i = j + d
                    if 0 <= i < 4:
                        js, cs = slice(j * BLOCK, (j + 1) * BLOCK), slice(i * BLOCK, (i + 1) * BLOCK)
                        probs = e_ref[h, js, cs] * r_ref[pl.ds(h, 1), cs]
                        ds = probs * (dp_ref[js, cs] - delta[i])
                        pb_ref[js, cs] = probs.astype(BF16)
                        dsb_ref[js, cs] = ds.astype(BF16)
                        diag = ds if diag is None else diag + ds
                strip = jnp.concatenate([jnp.zeros_like(diag), diag], axis=1)
                total = strip[0:8]
                for g in range(1, 16):
                    total = total + pltpu.roll(strip[8 * g : 8 * g + 8], 2 * BLOCK - 8 * g, 1)
                cs = slice((d + 2) * BLOCK, (d + 4) * BLOCK)
                g8_ref[:, cs] = g8_ref[:, cs] + total
            row = g8_ref[0:1, :]
            for s in range(1, 8):
                row = row + pltpu.roll(g8_ref[s : s + 1, :], WIDE - s, 1)
            gb_ref[pl.ds(h, 1), :] = row
            side = slice(64 * odd, 64 * odd + 64)
            dqt_ref[side, :] = nn(kpt[side, :], dsb_ref[...])
            dk_h, dv_h = nn(dsb_ref[...], qp), nn(pb_ref[...], gp)
            if odd == 0:
                dkp_ref[...] = dk_h
                dvp_ref[...] = dv_h
            else:
                dk_ref[:, columns(p)] = jnp.where(own, dk_h, dkp_ref[...]).astype(BF16)
                dv_ref[:, columns(p)] = jnp.where(own, dv_h, dvp_ref[...]).astype(BF16)
        dq_ref[:, columns(p)] = dqt_ref[...].T.astype(BF16)

    def term(k):
        z_at = zs(k)
        block = lax.dot_general(
            g_ref[:, pl.ds(pl.multiple_of(z_at * 512, 512), 512)],
            att_ref[...],
            (((0,), (0,)), ((), ())),
            preferred_element_type=F32,
        ).astype(BF16)
        ta_ref[z_at] = block[:, :HALF].reshape(2, 4, 64, HALF)
        tb_ref[z_at] = block[:, HALF:].reshape(2, 4, 64, HALF)

    def sum_a_hop(k, way, part):
        come = rap_ref if way == 1 else ram_ref
        z_at = zs(k if way == 1 else 8 - k)
        if ("sa", k, way, part) in got:
            got["sa", k, way, part].wait_recv()
            ta_ref[z_at, part] = (
                ta_ref[z_at, part].astype(F32) + come[k, part].astype(F32)
            ).astype(BF16)
        got["sa", k - 1, way, part] = wire.send(
            ta_ref.at[z_at, part], come.at[k - 1, part], at_z(1 if way == 1 else 7)
        )

    def sum_a_step(k):
        for part in range(2):
            for way in (1, -1):
                if k < 4 or (part == 0) == (way == 1):
                    sum_a_hop(k, way, part)

    def sum_a_x():
        for part in range(2):
            for way in (1, -1):
                got["sa", 0, way, part].wait_recv()
            full = (
                ta_ref[z, part].astype(F32) + rap_ref[0, part].astype(F32) + ram_ref[0, part].astype(F32)
            )
            saf_ref[part] = full
            sa_ref[part] = full.astype(BF16)
        for k in (1, 3, 2):
            got["sax", k] = wire.send(sa_ref.at[:, xs(k)], rax_ref.at[k - 1], at_x(k))

    def sum_a_y():
        full = saf_ref[:, x]
        for k in (1, 3, 2):
            got["sax", k].wait_recv()
            full = full + rax_ref[k - 1].astype(F32)
        saf_ref[:, x] = full
        say_ref[...] = full.astype(BF16)
        got["say"] = wire.send(say_ref.at[1 - yl], ray_ref, pair)

    def sum_a_end():
        got["say"].wait_recv()
        wg_ref[:, :HALF] = saf_ref[yl, x] + ray_ref[...].astype(F32)

    def part_b(part):
        return pl.ds(part * 4, 4)

    def sum_b_first():
        got["sb", 1, 1, 0] = wire.send(tb_ref.at[part_b(0), :, xs(2)], rbp_ref.at[1], at_x(1))
        got["sb", 1, 3, 1] = wire.send(tb_ref.at[part_b(1), :, xs(2)], rbm_ref.at[1], at_x(3))
        sum_b_hop(1, 1)
        sum_b_hop(3, 0)

    def sum_b_hop(way, part):
        come = rbp_ref if way == 1 else rbm_ref
        if ("sb", 1, way, part) in got:
            got["sb", 1, way, part].wait_recv()
            at = (part_b(part), slice(None), xs(way))
            tb_ref[at] = (tb_ref[at].astype(F32) + come[1].astype(F32)).astype(BF16)
        got["sb", 0, way, part] = wire.send(
            tb_ref.at[part_b(part), :, xs(way)],
            (come.at[0] if (part == 0) == (way == 1) else come.at[2]),
            at_x(way),
        )

    def sum_b_second():
        sum_b_hop(1, 0)
        sum_b_hop(3, 1)

    def sum_b_y():
        for part in (1, 0):
            for way in (1, 3):
                got["sb", 0, way, part].wait_recv()
        for part in range(2):
            up = rbp_ref[0 if part == 0 else 2].astype(F32)
            down = rbm_ref[2 if part == 0 else 0].astype(F32)
            full = tb_ref[part_b(part), :, x].astype(F32) + up + down
            sbf_ref[part_b(part)] = full
            sby_ref[part_b(part)] = full.astype(BF16)
        got["sby"] = wire.send(sby_ref.at[:, 1 - yl], rby_ref, pair)

    def sum_b_z():
        got["sby"].wait_recv()
        full = sbf_ref[:, yl] + rby_ref[...].astype(F32)
        sbf_ref[:, 0] = full
        sbz_ref[...] = full.astype(BF16)
        for k in range(1, 8):
            got["sbz", k] = wire.send(sbz_ref.at[zs(k)], rbz_ref.at[k - 1], at_z(k))

    def sum_b_end():
        full = sbf_ref[z, 0]
        for k in range(1, 8):
            got["sbz", k].wait_recv()
            full = full + rbz_ref[k - 1].astype(F32)
        wg_ref[:, HALF:] = full

    def table_z():
        here = lax.dot_general(
            gb_ref[...], oh_ref[...], (((1,), (1,)), ((), ())),
            precision=lax.Precision.HIGHEST, preferred_element_type=F32,
        )
        tz_ref[...] = jnp.concatenate([here, jnp.zeros((HEADS, BLOCK - 32), F32)], axis=1)
        for k in range(1, 8):
            got["tz", k] = wire.send(tz_ref, rtz_ref.at[k - 1], at_z(k))

    def table_x():
        full = tz_ref[...]
        for k in range(1, 8):
            got["tz", k].wait_recv()
            full = full + rtz_ref[k - 1]
        tx_ref[...] = full
        for k in range(1, 4):
            got["tx", k] = wire.send(tx_ref, rtx_ref.at[k - 1], at_x(k))

    def table_y():
        full = tx_ref[...]
        for k in range(1, 4):
            got["tx", k].wait_recv()
            full = full + rtx_ref[k - 1]
        ty_ref[...] = full
        got["ty"] = wire.send(ty_ref, rty_ref, pair)

    def table_end():
        got["ty"].wait_recv()
        tg_ref[...] = (ty_ref[...] + rty_ref[...])[:, :32]

    prepare()
    gather_a2()
    gather_a3()
    gather_b2()
    softmax_pair(0)
    up_hand_on(0)
    gather_a_step(1)
    gather_b3()
    up_hand_on(1)
    softmax_pair(1)
    gather_a_step(2)
    up_share(0)
    softmax_pair(2)
    gather_b4(0)
    gather_a_step(3)
    gather_b4(1)
    up_share(1)
    softmax_pair(3)
    up_end()
    for k in (4, 3, 5):
        term(k)
        if k == 4:
            sum_a_step(4)
    for part in range(2):
        for way in (1, -1):
            if ("sa", 3, way, part) not in got:
                sum_a_hop(3, way, part)
    for k in (2, 6, 1, 7, 0):
        term(k)
    sum_b_first()
    for part, way in ((0, 1), (1, -1)):
        sum_a_hop(3, way, part)
    gather_a_end()
    context(0, 0)
    context(0, 1)
    gather_b_end()
    sum_a_step(2)
    context(1, 0)
    context(1, 1)
    sum_b_second()
    backward_pair(0)
    sum_a_step(1)
    backward_pair(1)
    sum_b_y()
    sum_a_x()
    backward_pair(2)
    sum_b_z()
    sum_a_y()
    backward_pair(3)
    table_z()
    sum_a_end()
    table_x()
    sum_b_end()
    table_y()
    table_end()
    wire.finish()


def on_device(queries, keys, values, attended, upstream, out_weight, bias_table, buckets, segments):
    shifted = jnp.pad(buckets, (129, WIDE - 129 - buckets.shape[0]), constant_values=-1)[None, :]
    anywhere = pl.BlockSpec(memory_space=pl.ANY)
    inside = pl.BlockSpec(memory_space=pltpu.VMEM)
    bf, f4 = (lambda *s: pltpu.VMEM(s, BF16)), (lambda *s: pltpu.VMEM(s, F32))
    dq, dk, dv, wg, tg = pl.pallas_call(
        kernel,
        out_shape=(
            jax.ShapeDtypeStruct((ROWS, FEAT), BF16),
            jax.ShapeDtypeStruct((ROWS, FEAT), BF16),
            jax.ShapeDtypeStruct((ROWS, FEAT), BF16),
            jax.ShapeDtypeStruct((64, FEAT), F32),
            jax.ShapeDtypeStruct((HEADS, 32), F32),
        ),
        in_specs=[anywhere] * 6 + [inside] * 3,
        out_specs=(inside,) * 5,
        scratch_shapes=[
            bf(ROWS, FEAT), bf(ROWS, FEAT), bf(ROWS, FEAT), bf(ROWS, FEAT),
            bf(ROWS, D), bf(ROWS, FEAT),
            bf(8, 2, 4, 64, HALF), bf(8, 2, 4, 64, HALF),
            bf(2, 32, D), bf(2, 32, D),
            bf(8, 2, 4, 64, HALF), bf(8, 2, 4, 64, HALF),
            bf(4, 2, 4, 64, HALF), bf(4, 2, 4, 64, HALF),
            bf(2, 4, 64, HALF), f4(2, 4, 64, HALF), bf(3, 2, 64, HALF), bf(64, HALF), bf(2, 64, HALF),
            bf(3, 4, 2, 64, HALF), bf(3, 4, 2, 64, HALF),
            bf(8, 2, 64, HALF), f4(8, 2, 64, HALF), bf(8, 64, HALF), bf(8, 64, HALF), bf(7, 64, HALF),
            f4(HEADS, ROWS, ROWS), f4(HEADS, ROWS), f4(ROWS, ROWS), bf(ROWS, ROWS), bf(ROWS, ROWS),
            f4(5, BLOCK, BLOCK), f4(HEADS, WIDE), f4(32, WIDE), f4(HEADS, WIDE), f4(8, WIDE),
            bf(ROWS, BLOCK), bf(ROWS, BLOCK), f4(BLOCK, ROWS), f4(ROWS, BLOCK), f4(ROWS, BLOCK),
            f4(HEADS, BLOCK), f4(7, HEADS, BLOCK), f4(HEADS, BLOCK), f4(3, HEADS, BLOCK),
            f4(HEADS, BLOCK), f4(HEADS, BLOCK),
            pltpu.SemaphoreType.DMA((7,)),
            pltpu.SemaphoreType.DMA((N_SEM,)),
            pltpu.SemaphoreType.DMA((N_SEM,)),
        ],
        compiler_params=pltpu.CompilerParams(
            collective_id=0, has_side_effects=True, vmem_limit_bytes=60 * 1024 * 1024
        ),
    )(
        queries, keys, values, attended, upstream, out_weight.T, bias_table.T, shifted, segments[None, :]
    )
    return dq, dk, dv, wg, tg.T


def solution(mesh):
    in_specs = (
        P("dp", "tensor"),
        P("dp", "tensor"),
        P("dp", "tensor"),
        P("dp", "tensor"),
        P(("dp", "tensor"), None),
        P("tensor", "dp"),
        P(None, "tensor"),
        P(),
        P("dp"),
    )
    out_specs = (
        P("dp", "tensor"),
        P("dp", "tensor"),
        P("dp", "tensor"),
        P("dp", "tensor"),
        P(None, "tensor"),
    )
    return jax.shard_map(
        on_device, mesh=mesh, in_specs=in_specs, out_specs=out_specs, check_vma=False
    )
```

```python
import functools

import jax
import jax.numpy as jnp
from jax import lax
from jax.experimental import pallas as pl
from jax.experimental.pallas import tpu as pltpu
from jax.sharding import PartitionSpec as P

MESH = pl.DeviceIdType.MESH
F32 = jnp.float32
BF16 = jnp.bfloat16
ROWS = 512
FEAT = 512
HALF = 256
D = 4096
HEADS = 8
WIDE = 768
BLOCK = 128
FAR = -4096.0
N_SEM = 176
UP_CUTS = 4
UP_ROWS = 16


def nt(a, b):
    return lax.dot_general(a, b, (((1,), (1,)), ((), ())), preferred_element_type=F32)


def nn(a, b):
    return jnp.dot(a, b, preferred_element_type=F32)


class Wire:
    def __init__(self, send_sem, recv_sem):
        self.send_sem, self.recv_sem = send_sem, recv_sem
        self.made = []

    def send(self, src, dst, device):
        at = len(self.made)
        copy = pltpu.make_async_remote_copy(
            src_ref=src,
            dst_ref=dst,
            send_sem=self.send_sem.at[at],
            recv_sem=self.recv_sem.at[at],
            device_id=device,
            device_id_type=MESH,
        )
        copy.start()
        self.made.append(copy)
        return copy

    def finish(self):
        for copy in self.made:
            copy.wait_send()


def kernel(
    q_hbm, k_hbm, v_hbm, att_hbm, up_hbm, wt_hbm, table_ref, bucket_ref, seg_ref,
    dq_ref, dk_ref, dv_ref, wg_ref, tg_ref,
    q_ref, k_ref, v_ref, att_ref, g_ref, ctx_ref, wa_ref, wb_ref, fp_ref, fm_ref,
    ta_ref, tc_ref, tb_ref,
    rap_ref, ram_ref, sa_ref, saf_ref, rax_ref, ray_ref, say_ref,
    rcy_ref, rcp_ref, rcm_ref, sc_ref, scf_ref, rcx_ref,
    rbp_ref, rbm_ref, sby_ref, sbf_ref, rby_ref, sbz_ref, rbz_ref,
    e_ref, r_ref, dp_ref, pb_ref, dsb_ref, toe_ref, bext_ref, oh_ref, gb_ref, g8_ref,
    qaug_ref, kaug_ref, dqt_ref, dkp_ref, dvp_ref,
    tz_ref, rtz_ref, tx_ref, rtx_ref, ty_ref, rty_ref,
    local_sem, send_sem, recv_sem,
):
    me, tensor = lax.axis_index("dp"), lax.axis_index("tensor")
    x, yl, z = lax.rem(me, 4), lax.rem(lax.div(me, 4), 2), lax.div(me, 8)
    core, yh = lax.rem(tensor, 2), lax.div(tensor, 2)
    y = yh * 2 + yl

    def place(z_at, yl_at, x_at, yh_at, core_at):
        return {"dp": z_at * 8 + yl_at * 4 + x_at, "tensor": yh_at * 2 + core_at}

    def xs(k):
        return lax.rem(x + k, 4)

    def zs(k):
        return lax.rem(z + k, 8)

    def at_x(k):
        return place(z, yl, xs(k), yh, core)

    def at_z(k):
        return place(zs(k), yl, x, yh, core)

    def at_y(k):
        there = lax.rem(y + k, 4)
        return place(z, lax.rem(there, 2), x, lax.div(there, 2), core)

    pair = place(z, 1 - yl, x, yh, core)
    mate = place(z, yl, x, yh, 1 - core)

    loads = []
    for at, (src, dst) in enumerate(
        [
            (q_hbm, q_ref),
            (k_hbm, k_ref),
            (v_hbm, v_ref),
            (att_hbm, att_ref),
            (up_hbm, g_ref.at[pl.ds(pl.multiple_of(tensor * 128, 128), 128), :]),
            (wt_hbm.at[:, pl.ds(0, HALF)], wa_ref.at[z, yl, x]),
            (wt_hbm.at[:, pl.ds(HALF, HALF)], wb_ref.at[z, yl, x]),
        ]
    ):
        copy = pltpu.make_async_copy(src, dst, local_sem.at[at])
        copy.start()
        loads.append(copy)

    barrier = pltpu.get_barrier_semaphore()
    greeted = [at_z(k) for k in range(1, 8)] + [at_x(k) for k in range(1, 4)] + [at_y(1), at_y(3), mate]
    for device in greeted:
        pl.semaphore_signal(barrier, inc=1, device_id=device, device_id_type=MESH)
    pl.semaphore_wait(barrier, len(greeted))

    wire = Wire(send_sem, recv_sem)
    got = {}

    y_a = wire.send(wt_hbm.at[:, pl.ds(0, HALF)], wa_ref.at[z, yl, x], pair)
    y_b = wire.send(wt_hbm.at[:, pl.ds(HALF, HALF)], wb_ref.at[z, yl, x], pair)
    up_fp, up_fm = [], []
    for c in range(UP_CUTS):
        up_fp.append(wire.send(up_hbm.at[pl.ds(c * UP_ROWS, UP_ROWS), :], fp_ref.at[c], at_y(1)))
        up_fm.append(wire.send(up_hbm.at[pl.ds(64 + c * UP_ROWS, UP_ROWS), :], fm_ref.at[c], at_y(3)))
    own_rows = pl.multiple_of(tensor * 128, 128)
    to_mate = [wire.send(up_hbm, g_ref.at[pl.ds(own_rows, 128), :], mate)]
    for copy in loads:
        copy.wait()

    before = lax.div(lax.rem(y + 3, 4), 2) * 2 + core
    after = lax.div(lax.rem(y + 1, 4), 2) * 2 + core
    across = (1 - yh) * 2 + core

    def gather_first():
        y_a.wait_recv()
        y_b.wait_recv()
        got["a_x"] = [wire.send(wa_ref.at[z, :, x], wa_ref.at[z, :, x], at_x(k)) for k in (1, 3, 2)]
        for way in (1, -1):
            got["b_z", 1, way] = b_hop(1, way)
        b_spread(0)

    def far(step, way):
        return zs(8 - step if way == 1 else step)

    def z_next(way):
        return at_z(1 if way == 1 else 7)

    def a_hop(step, way, part):
        chunk = wa_ref.at[far(step - 1, way), part]
        return wire.send(chunk, chunk, z_next(way))

    def gather_a_start():
        for copy in got["a_x"]:
            copy.wait_recv()
        for part in range(2):
            for way in (1, -1):
                got["a_z", 1, way, part] = a_hop(1, way, part)

    def gather_a_step(step):
        for part in range(2):
            for way in (1, -1):
                got["a_z", step, way, part].wait_recv()
                if step < 3 or (part == 0) == (way == 1):
                    got["a_z", step + 1, way, part] = a_hop(step + 1, way, part)

    def gather_a_end():
        got["a_z", 4, 1, 0].wait_recv()
        got["a_z", 4, -1, 1].wait_recv()

    def b_hop(step, way):
        chunk = wb_ref.at[far(step - 1, way), :, x]
        return wire.send(chunk, chunk, z_next(way))

    def b_half_hop(way):
        chunk = wb_ref.at[far(3, way), 0 if way == 1 else 1, x]
        return wire.send(chunk, chunk, z_next(way))

    def b_spread(k):
        chunk = wb_ref.at[zs(k), :, x]
        for side in (1, 3):
            got["b_x", k, side] = wire.send(chunk, chunk, at_x(side))

    def gather_b_step(step):
        for way in (1, -1):
            if step < 4:
                got["b_z", step, way].wait_recv()
            else:
                got["b_z", 4, way].wait_recv()
            if step < 3:
                got["b_z", step + 1, way] = b_hop(step + 1, way)
            elif step == 3:
                got["b_z", 4, way] = b_half_hop(way)
            if step < 4:
                b_spread(8 - step if way == 1 else step)
        if step == 4:
            b_spread(4)

    def gather_b_across(k):
        for side in (1, 3):
            got["b_x", k, side].wait_recv()
            chunk = wb_ref.at[zs(k), 0 if side == 1 else 1, xs(3 if side == 1 else 1)]
            got["b_x2", k, side] = wire.send(chunk, chunk, at_x(side))

    def gather_b_end():
        for k in range(8):
            for side in (1, 3):
                got["b_x2", k, side].wait_recv()

    def rows_of(owner, first):
        return g_ref.at[pl.ds(pl.multiple_of(owner * 128 + first, UP_ROWS), UP_ROWS), :]

    def up_hand_on(c):
        up_fp[c].wait_recv()
        got["u", 0, c] = wire.send(fp_ref.at[c], rows_of(before, c * UP_ROWS), at_y(1))
        up_fm[c].wait_recv()
        got["u", 1, c] = wire.send(fm_ref.at[c], rows_of(after, 64 + c * UP_ROWS), at_y(3))

    def up_share(c):
        for side in range(2):
            got["u", side, c].wait_recv()
            block = rows_of(across, side * 64 + c * UP_ROWS)
            to_mate.append(wire.send(block, block, mate))

    def up_end():
        for copy in to_mate:
            copy.wait_recv()

    def prepare():
        lane = lax.broadcasted_iota(jnp.int32, (ROWS, BLOCK), 1)
        spot = jnp.where(lane < 64, lane, lane - 64)
        seg = jnp.broadcast_to(seg_ref[...].astype(F32), (BLOCK, ROWS)).T
        same = seg == spot.astype(F32)
        qaug_ref[...] = jnp.where(same, 1.0, 0.0).astype(BF16)
        kaug_ref[...] = jnp.where((spot < 3) & jnp.logical_not(same), FAR, 0.0).astype(BF16)
        oh_ref[...] = jnp.where(
            lax.broadcasted_iota(jnp.int32, (32, WIDE), 0) == bucket_ref[...], 1.0, 0.0
        )
        bext_ref[...] = jnp.dot(
            table_ref[...], oh_ref[...], precision=lax.Precision.HIGHEST, preferred_element_type=F32
        )
        pb_ref[...] = jnp.zeros_like(pb_ref)
        dsb_ref[...] = jnp.zeros_like(dsb_ref)

    def columns(p):
        return pl.ds(p * BLOCK, BLOCK)

    def own_lanes(odd):
        lane = lax.broadcasted_iota(jnp.int32, (ROWS, BLOCK), 1)
        return (lane >= 64) if odd else (lane < 64)

    def softmax_head(h):
        p, odd = h // 2, h % 2
        qp, kp = q_ref[:, columns(p)], k_ref[:, columns(p)]
        if True:
            own = own_lanes(odd)
            q_h = jnp.where(own, qp, qaug_ref[...])
            k_h = jnp.where(own, kp, kaug_ref[...])
            bias = bext_ref[pl.ds(h, 1), :]
            for d in range(5):
                strip = jnp.broadcast_to(bias[:, d * BLOCK : (d + 2) * BLOCK], (BLOCK, 2 * BLOCK))
                toe_ref[d] = pltpu.roll(strip, 0, 1, stride=1, stride_axis=0)[:, BLOCK:]
            for i2 in range(2):
                peak = [None, None]
                for j in range(4):
                    s2 = nt(k_h[j * BLOCK : (j + 1) * BLOCK], q_h[i2 * 256 : (i2 + 1) * 256])
                    for sub in range(2):
                        i = 2 * i2 + sub
                        if abs(i - j) <= 2:
                            s = s2[:, sub * BLOCK : (sub + 1) * BLOCK] + toe_ref[i - j + 2]
                            e_ref[h, j * BLOCK : (j + 1) * BLOCK, i * BLOCK : (i + 1) * BLOCK] = s
                            top = jnp.max(s.reshape(16, 8, BLOCK), axis=0)
                            peak[sub] = top if peak[sub] is None else jnp.maximum(peak[sub], top)
                for sub in range(2):
                    i = 2 * i2 + sub
                    top = jnp.max(peak[sub], axis=0, keepdims=True)
                    total = None
                    for j in range(4):
                        if abs(i - j) <= 2:
                            at = (h, slice(j * BLOCK, (j + 1) * BLOCK), slice(i * BLOCK, (i + 1) * BLOCK))
                            e = jnp.exp(e_ref[at] - top)
                            e_ref[at] = e
                            part = jnp.sum(e.reshape(16, 8, BLOCK), axis=0)
                            total = part if total is None else total + part
                    r_ref[pl.ds(h, 1), i * BLOCK : (i + 1) * BLOCK] = 1.0 / jnp.sum(
                        total, axis=0, keepdims=True
                    )

    def context(which, m):
        w = (wa_ref if which == 0 else wb_ref)[...].reshape(D, HALF)
        rows = slice(m * 256, (m + 1) * 256)
        ctx_ref[rows, which * HALF : (which + 1) * HALF] = nn(g_ref[rows, :], w).astype(BF16)

    def backward_head(h):
        p, odd = h // 2, h % 2
        qp, kp = q_ref[:, columns(p)], k_ref[:, columns(p)]
        vp, gp = v_ref[:, columns(p)], ctx_ref[:, columns(p)]
        kpt = kp.T
        if True:
            own = own_lanes(odd)
            g_h = jnp.where(own, gp, jnp.zeros_like(gp))
            delta = []
            for i2 in range(2):
                sums = [None, None]
                for j in range(4):
                    d2 = nt(vp[j * BLOCK : (j + 1) * BLOCK], g_h[i2 * 256 : (i2 + 1) * 256])
                    for sub in range(2):
                        i = 2 * i2 + sub
                        if abs(i - j) <= 2:
                            js, cs = slice(j * BLOCK, (j + 1) * BLOCK), slice(i * BLOCK, (i + 1) * BLOCK)
                            d1 = d2[:, sub * BLOCK : (sub + 1) * BLOCK]
                            dp_ref[js, cs] = d1
                            part = jnp.sum((e_ref[h, js, cs] * d1).reshape(16, 8, BLOCK), axis=0)
                            sums[sub] = part if sums[sub] is None else sums[sub] + part
                for sub in range(2):
                    i = 2 * i2 + sub
                    recip = r_ref[pl.ds(h, 1), i * BLOCK : (i + 1) * BLOCK]
                    delta.append(recip * jnp.sum(sums[sub], axis=0, keepdims=True))
            g8_ref[...] = jnp.zeros_like(g8_ref)
            for d in range(-2, 3):
                diag = None
                for j in range(4):
                    i = j + d
                    if 0 <= i < 4:
                        js, cs = slice(j * BLOCK, (j + 1) * BLOCK), slice(i * BLOCK, (i + 1) * BLOCK)
                        probs = e_ref[h, js, cs] * r_ref[pl.ds(h, 1), cs]
                        ds = probs * (dp_ref[js, cs] - delta[i])
                        pb_ref[js, cs] = probs.astype(BF16)
                        dsb_ref[js, cs] = ds.astype(BF16)
                        diag = ds if diag is None else diag + ds
                strip = jnp.concatenate([jnp.zeros_like(diag), diag], axis=1)
                total = strip[0:8]
                for g in range(1, 16):
                    total = total + pltpu.roll(strip[8 * g : 8 * g + 8], 2 * BLOCK - 8 * g, 1)
                cs = slice((d + 2) * BLOCK, (d + 4) * BLOCK)
                g8_ref[:, cs] = g8_ref[:, cs] + total
            row = g8_ref[0:1, :]
            for s in range(1, 8):
                row = row + pltpu.roll(g8_ref[s : s + 1, :], WIDE - s, 1)
            gb_ref[pl.ds(h, 1), :] = row
            side = slice(64 * odd, 64 * odd + 64)
            dqt_ref[side, :] = nn(kpt[side, :], dsb_ref[...])
            dk_h, dv_h = nn(dsb_ref[...], qp), nn(pb_ref[...], gp)
            if odd == 0:
                dkp_ref[...] = dk_h
                dvp_ref[...] = dv_h
            else:
                dk_ref[:, columns(p)] = jnp.where(own, dk_h, dkp_ref[...]).astype(BF16)
                dv_ref[:, columns(p)] = jnp.where(own, dv_h, dvp_ref[...]).astype(BF16)
        if odd == 1:
            dq_ref[:, columns(p)] = dqt_ref[...].T.astype(BF16)

    def term(k):
        z_at = zs(k)
        block = lax.dot_general(
            g_ref[:, pl.ds(pl.multiple_of(z_at * 512, 512), 512)],
            att_ref[...],
            (((0,), (0,)), ((), ())),
            preferred_element_type=F32,
        ).astype(BF16)
        ta_ref[z_at] = block[:, :BLOCK].reshape(2, 4, 64, BLOCK)
        tc_ref[z_at] = block[:, BLOCK:HALF].reshape(2, 4, 64, BLOCK)
        tb_ref[z_at] = block[:, HALF:].reshape(2, 4, 64, HALF)

    def total(*parts):
        out = parts[0].astype(F32)
        for part in parts[1:]:
            out = out + part.astype(F32)
        return out

    def sum_a_hop(k, way, part):
        come = rap_ref if way == 1 else ram_ref
        z_at = zs(k if way == 1 else 8 - k)
        if ("sa", k, way, part) in got:
            got["sa", k, way, part].wait_recv()
            ta_ref[z_at, part] = total(ta_ref[z_at, part], come[k, part]).astype(BF16)
        got["sa", k - 1, way, part] = wire.send(
            ta_ref.at[z_at, part], come.at[k - 1, part], z_next(way)
        )

    def sum_a_step(k):
        for part in range(2):
            for way in (1, -1):
                sum_a_hop(k, way, part)

    def sum_a_x(part):
        for way in (1, -1):
            got["sa", 0, way, part].wait_recv()
        full = total(ta_ref[z, part], rap_ref[0, part], ram_ref[0, part])
        saf_ref[part] = full
        sa_ref[part] = full.astype(BF16)
        for k in (2, 1, 3):
            got["sax", part, k] = wire.send(sa_ref.at[part, xs(k)], rax_ref.at[part, k - 1], at_x(k))

    def sum_a_y():
        for part in range(2):
            full = saf_ref[part, x]
            for k in (1, 3, 2):
                got["sax", part, k].wait_recv()
                full = full + rax_ref[part, k - 1].astype(F32)
            saf_ref[part, x] = full
            say_ref[part] = full.astype(BF16)
        got["say"] = wire.send(say_ref.at[1 - yl], ray_ref, pair)

    def sum_a_end():
        got["say"].wait_recv()
        wg_ref[:, :BLOCK] = total(saf_ref[yl, x], ray_ref[...])

    def sum_c_y(k):
        got["scy", k] = wire.send(tc_ref.at[zs(k), 1 - yl], rcy_ref.at[k], pair)

    def sum_c_hop(k, way):
        come = rcp_ref if way == 1 else rcm_ref
        rel = k if way == 1 else 8 - k
        got["scy", rel].wait_recv()
        parts = [tc_ref[zs(rel), yl], rcy_ref[rel]]
        if ("sc", k, way) in got:
            got["sc", k, way].wait_recv()
            parts.append(come[k])
        tc_ref[zs(rel), yl] = total(*parts).astype(BF16)
        got["sc", k - 1, way] = wire.send(tc_ref.at[zs(rel), yl], come.at[k - 1], z_next(way))

    def sum_c_step(k):
        for way in (1, -1):
            sum_c_hop(k, way)

    def sum_c_x():
        got["scy", 0].wait_recv()
        for way in (1, -1):
            got["sc", 0, way].wait_recv()
        full = total(tc_ref[z, yl], rcy_ref[0], rcp_ref[0], rcm_ref[0])
        scf_ref[...] = full
        sc_ref[...] = full.astype(BF16)
        for k in (2, 1, 3):
            got["scx", k] = wire.send(sc_ref.at[xs(k)], rcx_ref.at[k - 1], at_x(k))

    def sum_c_end():
        full = scf_ref[x]
        for k in (1, 3, 2):
            got["scx", k].wait_recv()
            full = full + rcx_ref[k - 1].astype(F32)
        wg_ref[:, BLOCK:HALF] = full

    def sum_b_first(k, side):
        other = 4 - side
        come = rbp_ref if side == 1 else rbm_ref
        back = rbm_ref if side == 1 else rbp_ref
        got["sb2", k] = wire.send(tb_ref.at[zs(k), :, xs(2)], come.at[k, 1], at_x(side))
        got["sb1", k, other] = wire.send(tb_ref.at[zs(k), :, xs(other)], back.at[k, 0], at_x(other))

    def sum_b_second(k, side):
        come = rbp_ref if side == 1 else rbm_ref
        got["sb2", k].wait_recv()
        at = (zs(k), slice(None), xs(side))
        tb_ref[at] = total(tb_ref[at], come[k, 1]).astype(BF16)
        got["sb1", k, side] = wire.send(tb_ref.at[at], come.at[k, 0], at_x(side))

    def sum_b_y(k):
        for side in (1, 3):
            got["sb1", k, side].wait_recv()
        full = total(tb_ref[zs(k), :, x], rbp_ref[k, 0], rbm_ref[k, 0])
        sbf_ref[k] = full
        sby_ref[k] = full.astype(BF16)
        got["sby", k] = wire.send(sby_ref.at[k, 1 - yl], rby_ref.at[k], pair)

    def sum_b_z(k):
        got["sby", k].wait_recv()
        full = total(sbf_ref[k, yl], rby_ref[k])
        if k:
            sbz_ref[k] = full.astype(BF16)
            got["sbz", k] = wire.send(sbz_ref.at[k], rbz_ref.at[k - 1], at_z(k))
        else:
            sbf_ref[0, 0] = full

    def sum_b_end():
        full = sbf_ref[0, 0]
        for k in range(1, 8):
            got["sbz", k].wait_recv()
            full = full + rbz_ref[k - 1].astype(F32)
        wg_ref[:, HALF:] = full

    def table_z():
        here = lax.dot_general(
            gb_ref[...], oh_ref[...], (((1,), (1,)), ((), ())),
            precision=lax.Precision.HIGHEST, preferred_element_type=F32,
        )
        tz_ref[...] = jnp.concatenate([here, jnp.zeros((HEADS, BLOCK - 32), F32)], axis=1)
        for k in range(1, 8):
            got["tz", k] = wire.send(tz_ref, rtz_ref.at[k - 1], at_z(k))

    def table_x():
        full = tz_ref[...]
        for k in range(1, 8):
            got["tz", k].wait_recv()
            full = full + rtz_ref[k - 1]
        tx_ref[...] = full
        for k in range(1, 4):
            got["tx", k] = wire.send(tx_ref, rtx_ref.at[k - 1], at_x(k))

    def table_y():
        full = tx_ref[...]
        for k in range(1, 4):
            got["tx", k].wait_recv()
            full = full + rtx_ref[k - 1]
        ty_ref[...] = full
        got["ty"] = wire.send(ty_ref, rty_ref, pair)

    def table_end():
        got["ty"].wait_recv()
        tg_ref[...] = (ty_ref[...] + rty_ref[...])[:, :32]

    prepare()
    gather_first()
    softmax_head(0)
    up_hand_on(0)
    gather_a_start()
    gather_b_step(1)
    gather_b_across(0)
    softmax_head(1)
    up_hand_on(1)
    softmax_head(2)
    up_hand_on(2)
    gather_b_step(2)
    softmax_head(3)
    gather_b_across(1)
    gather_b_across(7)
    up_hand_on(3)
    gather_a_step(1)
    softmax_head(4)
    gather_b_step(3)
    up_share(0)
    softmax_head(5)
    gather_b_across(2)
    gather_b_across(6)
    up_share(1)
    gather_b_step(4)
    gather_a_step(2)
    softmax_head(6)
    up_share(2)
    gather_b_across(3)
    gather_b_across(5)
    softmax_head(7)
    up_share(3)
    up_end()
    term(4)
    sum_a_hop(4, 1, 0)
    sum_a_hop(4, -1, 1)
    sum_c_y(4)
    sum_b_first(4, 1)
    gather_a_step(3)
    gather_b_across(4)
    term(3)
    sum_a_hop(3, 1, 1)
    sum_c_y(3)
    sum_b_first(3, 3)
    term(5)
    sum_a_hop(3, -1, 0)
    sum_c_y(5)
    sum_b_first(5, 1)
    term(2)
    sum_c_y(2)
    sum_b_first(2, 3)
    sum_a_hop(3, 1, 0)
    sum_a_hop(3, -1, 1)
    sum_c_hop(4, 1)
    for k, side in ((6, 1), (1, 3), (7, 1), (0, 3)):
        term(k)
        sum_c_y(k)
        sum_b_first(k, side)
    gather_a_end()
    context(0, 0)
    context(0, 1)
    sum_a_step(2)
    sum_c_step(3)
    sum_b_second(4, 1)
    sum_b_second(3, 3)
    gather_b_end()
    context(1, 0)
    context(1, 1)
    backward_head(0)
    sum_a_step(1)
    sum_c_step(2)
    sum_b_second(5, 1)
    sum_b_second(2, 3)
    backward_head(1)
    backward_head(2)
    sum_b_second(6, 1)
    sum_b_second(1, 3)
    sum_c_step(1)
    sum_a_x(0)
    sum_a_x(1)
    backward_head(3)
    sum_b_second(7, 1)
    sum_b_second(0, 3)
    sum_b_y(4)
    sum_b_y(3)
    backward_head(4)
    sum_c_x()
    sum_a_y()
    sum_b_y(5)
    sum_b_y(2)
    sum_b_z(4)
    sum_b_z(3)
    backward_head(5)
    sum_b_y(6)
    sum_b_y(1)
    sum_b_z(5)
    sum_b_z(2)
    sum_b_y(7)
    sum_b_y(0)
    backward_head(6)
    sum_b_z(6)
    sum_b_z(1)
    backward_head(7)
    table_z()
    sum_b_z(7)
    sum_b_z(0)
    sum_c_end()
    sum_a_end()
    table_x()
    sum_b_end()
    table_y()
    table_end()
    wire.finish()


def carry(*refs):
    sems = refs[-1]
    pairs = zip(refs[:5], refs[5:10])
    copies = [pltpu.make_async_copy(src, dst, sems.at[at]) for at, (src, dst) in enumerate(pairs)]
    for copy in copies:
        copy.start()
    for copy in copies:
        copy.wait()


def on_device(queries, keys, values, attended, upstream, out_weight, bias_table, buckets, segments):
    shifted = jnp.pad(buckets, (129, WIDE - 129 - buckets.shape[0]), constant_values=-1)[None, :]
    anywhere = pl.BlockSpec(memory_space=pl.ANY)
    inside = pl.BlockSpec(memory_space=pltpu.VMEM)
    bf, f4 = (lambda *s: pltpu.VMEM(s, BF16)), (lambda *s: pltpu.VMEM(s, F32))
    shapes = (
        jax.ShapeDtypeStruct((ROWS, FEAT), BF16),
        jax.ShapeDtypeStruct((ROWS, FEAT), BF16),
        jax.ShapeDtypeStruct((ROWS, FEAT), BF16),
        jax.ShapeDtypeStruct((64, FEAT), F32),
        jax.ShapeDtypeStruct((HEADS, 32), F32),
    )
    made = pl.pallas_call(
        kernel,
        out_shape=shapes,
        in_specs=[anywhere] * 6 + [inside] * 3,
        out_specs=(inside,) * 5,
        scratch_shapes=[
            bf(ROWS, FEAT), bf(ROWS, FEAT), bf(ROWS, FEAT), bf(ROWS, FEAT),
            bf(ROWS, D), bf(ROWS, FEAT),
            bf(8, 2, 4, 64, HALF), bf(8, 2, 4, 64, HALF),
            bf(UP_CUTS, UP_ROWS, D), bf(UP_CUTS, UP_ROWS, D),
            bf(8, 2, 4, 64, BLOCK), bf(8, 2, 4, 64, BLOCK), bf(8, 2, 4, 64, HALF),
            bf(4, 2, 4, 64, BLOCK), bf(4, 2, 4, 64, BLOCK), bf(2, 4, 64, BLOCK), f4(2, 4, 64, BLOCK),
            bf(2, 3, 64, BLOCK), bf(64, BLOCK), bf(2, 64, BLOCK),
            bf(8, 4, 64, BLOCK), bf(4, 4, 64, BLOCK), bf(4, 4, 64, BLOCK), bf(4, 64, BLOCK),
            f4(4, 64, BLOCK), bf(3, 64, BLOCK),
            bf(8, 2, 2, 64, HALF), bf(8, 2, 2, 64, HALF), bf(8, 2, 64, HALF), f4(8, 2, 64, HALF),
            bf(8, 64, HALF), bf(8, 64, HALF), bf(7, 64, HALF),
            f4(HEADS, ROWS, ROWS), f4(HEADS, ROWS), f4(ROWS, ROWS), bf(ROWS, ROWS), bf(ROWS, ROWS),
            f4(5, BLOCK, BLOCK), f4(HEADS, WIDE), f4(32, WIDE), f4(HEADS, WIDE), f4(8, WIDE),
            bf(ROWS, BLOCK), bf(ROWS, BLOCK), f4(BLOCK, ROWS), f4(ROWS, BLOCK), f4(ROWS, BLOCK),
            f4(HEADS, BLOCK), f4(7, HEADS, BLOCK), f4(HEADS, BLOCK), f4(3, HEADS, BLOCK),
            f4(HEADS, BLOCK), f4(HEADS, BLOCK),
            pltpu.SemaphoreType.DMA((7,)),
            pltpu.SemaphoreType.DMA((N_SEM,)),
            pltpu.SemaphoreType.DMA((N_SEM,)),
        ],
        compiler_params=pltpu.CompilerParams(
            collective_id=0, has_side_effects=True, vmem_limit_bytes=60 * 1024 * 1024
        ),
    )(
        queries, keys, values, attended, upstream, out_weight.T, bias_table.T, shifted, segments[None, :]
    )
    dq, dk, dv, wg, tg = pl.pallas_call(
        carry,
        out_shape=shapes,
        in_specs=[anywhere] * 5,
        out_specs=(anywhere,) * 5,
        scratch_shapes=[pltpu.SemaphoreType.DMA((5,))],
    )(*made)
    return dq, dk, dv, wg, tg.T


def solution(mesh):
    in_specs = (
        P("dp", "tensor"),
        P("dp", "tensor"),
        P("dp", "tensor"),
        P("dp", "tensor"),
        P(("dp", "tensor"), None),
        P("tensor", "dp"),
        P(None, "tensor"),
        P(),
        P("dp"),
    )
    out_specs = (
        P("dp", "tensor"),
        P("dp", "tensor"),
        P("dp", "tensor"),
        P("dp", "tensor"),
        P(None, "tensor"),
    )
    return jax.shard_map(
        on_device, mesh=mesh, in_specs=in_specs, out_specs=out_specs, check_vma=False
    )
```

```python
import jax
import jax.numpy as jnp
from jax import lax
from jax.experimental import pallas as pl
from jax.experimental.pallas import tpu as pltpu
from jax.sharding import PartitionSpec as P

MESH = pl.DeviceIdType.MESH
F32 = jnp.float32
BF16 = jnp.bfloat16
ROWS = 512
FEAT = 512
HALF = 256
D = 4096
HEADS = 8
WIDE = 768
BLOCK = 128
FAR = -4096.0
N_SEM = 224
KS = (4, 3, 5, 2, 6, 1, 7, 0)
WINDOW = 3


def nt(a, b):
    return lax.dot_general(a, b, (((1,), (1,)), ((), ())), preferred_element_type=F32)


def nn(a, b):
    return jnp.dot(a, b, preferred_element_type=F32)


class Wire:
    def __init__(self, send_sem, recv_sem):
        self.send_sem, self.recv_sem = send_sem, recv_sem
        self.made = []

    def send(self, src, dst, device):
        at = len(self.made)
        copy = pltpu.make_async_remote_copy(
            src_ref=src,
            dst_ref=dst,
            send_sem=self.send_sem.at[at],
            recv_sem=self.recv_sem.at[at],
            device_id=device,
            device_id_type=MESH,
        )
        copy.start()
        self.made.append(copy)
        return copy

    def finish(self):
        for copy in self.made:
            copy.wait_send()


def kernel(
    q_hbm, k_hbm, v_hbm, att_hbm, up_hbm, wt_hbm, table_ref, bucket_ref, seg_ref,
    dq_ref, dk_ref, dv_ref, wg_ref, tg_ref,
    q_ref, k_ref, v_ref, att_ref, g_ref, ctx_ref, wa_ref, wb_ref, fp_ref, fm_ref,
    ta_ref, tc_ref, tb_ref,
    rap_ref, ram_ref, sa_ref, saf_ref, rax_ref, ray_ref, say_ref,
    rcy_ref, rcp_ref, rcm_ref, sc_ref, scf_ref, rcx_ref,
    rbp_ref, rbm_ref, sby_ref, sbf_ref, rby_ref, sbz_ref, rbz_ref,
    e_ref, r_ref, dp_ref, pb_ref, dsb_ref, toe_ref, bext_ref, oh_ref, gb_ref, g8_ref,
    qaug_ref, kaug_ref, dqt_ref, dkp_ref, dvp_ref,
    tz_ref, rtz_ref, tx_ref, rtx_ref,
    local_sem, send_sem, recv_sem,
):
    me, tensor = lax.axis_index("dp"), lax.axis_index("tensor")
    x, yl, z = lax.rem(me, 4), lax.rem(lax.div(me, 4), 2), lax.div(me, 8)
    core, yh = lax.rem(tensor, 2), lax.div(tensor, 2)
    y = yh * 2 + yl

    def place(z_at, yl_at, x_at, yh_at, core_at):
        return {"dp": z_at * 8 + yl_at * 4 + x_at, "tensor": yh_at * 2 + core_at}

    def xs(k):
        return lax.rem(x + k, 4)

    def zs(k):
        return lax.rem(z + k, 8)

    def at_x(k):
        return place(z, yl, xs(k), yh, core)

    def at_z(k):
        return place(zs(k), yl, x, yh, core)

    def at_y(k):
        there = lax.rem(y + k, 4)
        return place(z, lax.rem(there, 2), x, lax.div(there, 2), core)

    pair = place(z, 1 - yl, x, yh, core)
    mate = place(z, yl, x, yh, 1 - core)

    loads = []
    for at, (src, dst) in enumerate(
        [
            (q_hbm, q_ref),
            (k_hbm, k_ref),
            (v_hbm, v_ref),
            (att_hbm, att_ref),
            (up_hbm, g_ref.at[pl.ds(pl.multiple_of(tensor * 128, 128), 128), :]),
            (wt_hbm.at[:, pl.ds(0, HALF)], wa_ref.at[z, yl, x]),
            (wt_hbm.at[:, pl.ds(HALF, HALF)], wb_ref.at[z, yl, x]),
        ]
    ):
        copy = pltpu.make_async_copy(src, dst, local_sem.at[at])
        copy.start()
        loads.append(copy)

    barrier = pltpu.get_barrier_semaphore()
    around = [at_x(k) for k in range(1, 4)] + [place(z, 1 - yl, xs(k), yh, core) for k in range(4)]
    greeted = [at_z(k) for k in range(1, 8)] + around + [place(z, 1 - yl, x, 1 - yh, core), mate]
    for device in greeted:
        pl.semaphore_signal(barrier, inc=1, device_id=device, device_id_type=MESH)
    pl.semaphore_wait(barrier, len(greeted))

    wire = Wire(send_sem, recv_sem)
    got = {}

    y_a = wire.send(wt_hbm.at[:, pl.ds(0, HALF)], wa_ref.at[z, yl, x], pair)
    y_b = wire.send(wt_hbm.at[:, pl.ds(HALF, HALF)], wb_ref.at[z, yl, x], pair)
    up_fp, up_fm = {}, {}

    def cols(k):
        return pl.ds(pl.multiple_of(zs(k) * FEAT, FEAT), FEAT)

    def up_first(i):
        up_fp[i] = wire.send(up_hbm.at[pl.ds(0, 64), cols(KS[i])], fp_ref.at[i], at_y(1))
        up_fm[i] = wire.send(up_hbm.at[pl.ds(64, 64), cols(KS[i])], fm_ref.at[i], at_y(3))

    for i in range(WINDOW):
        up_first(i)
    own_rows = pl.multiple_of(tensor * 128, 128)
    to_mate = wire.send(up_hbm, g_ref.at[pl.ds(own_rows, 128), :], mate)
    for copy in loads:
        copy.wait()

    before = lax.div(lax.rem(y + 3, 4), 2) * 2 + core
    after = lax.div(lax.rem(y + 1, 4), 2) * 2 + core
    across = (1 - yh) * 2 + core

    def gather_first():
        y_a.wait_recv()
        y_b.wait_recv()
        got["a_x"] = [wire.send(wa_ref.at[z, :, x], wa_ref.at[z, :, x], at_x(k)) for k in (1, 3, 2)]
        for way in (1, -1):
            got["b_z", 1, way] = b_hop(1, way)
            got["a_z", 1, way, 0] = a_hop(1, way, 0)
        b_spread(0)

    def far(step, way):
        return zs(8 - step if way == 1 else step)

    def z_next(way):
        return at_z(1 if way == 1 else 7)

    def a_hop(step, way, part):
        chunk = wa_ref.at[far(step - 1, way), :, xs(part)]
        return wire.send(chunk, chunk, z_next(way))

    def gather_a_start():
        for copy, part in zip(got["a_x"], (3, 1, 2)):
            copy.wait_recv()
            for way in (1, -1):
                got["a_z", 1, way, part] = a_hop(1, way, part)

    def gather_a_step(step):
        for part in (0, 3, 1, 2):
            for way in (1, -1):
                got["a_z", step, way, part].wait_recv()
                if step < 3 or (part in (0, 3)) == (way == 1):
                    got["a_z", step + 1, way, part] = a_hop(step + 1, way, part)

    def gather_a_end():
        for part, way in ((0, 1), (3, 1), (1, -1), (2, -1)):
            got["a_z", 4, way, part].wait_recv()

    def b_hop(step, way):
        chunk = wb_ref.at[far(step - 1, way), :, x]
        return wire.send(chunk, chunk, z_next(way))

    def b_half_hop(way):
        chunk = wb_ref.at[far(3, way), 0 if way == 1 else 1, x]
        return wire.send(chunk, chunk, z_next(way))

    def b_spread(k):
        chunk = wb_ref.at[zs(k), :, x]
        for side in (1, 3):
            got["b_x", k, side] = wire.send(chunk, chunk, at_x(side))

    def gather_b_step(step):
        for way in (1, -1):
            if step < 4:
                got["b_z", step, way].wait_recv()
            else:
                got["b_z", 4, way].wait_recv()
            if step < 3:
                got["b_z", step + 1, way] = b_hop(step + 1, way)
            elif step == 3:
                got["b_z", 4, way] = b_half_hop(way)
            if step < 4:
                b_spread(8 - step if way == 1 else step)
        if step == 4:
            b_spread(4)

    def gather_b_across(k):
        for side in (1, 3):
            got["b_x", k, side].wait_recv()
            chunk = wb_ref.at[zs(k), 0 if side == 1 else 1, xs(3 if side == 1 else 1)]
            got["b_x2", k, side] = wire.send(chunk, chunk, at_x(side))

    def gather_b_end():
        for k in range(8):
            for side in (1, 3):
                got["b_x2", k, side].wait_recv()

    def block_of(owner, first, k):
        return g_ref.at[pl.ds(pl.multiple_of(owner * 128 + first, 64), 64), cols(k)]

    def up_hand_on(i):
        up_fp[i].wait_recv()
        got["u", 0, i] = wire.send(fp_ref.at[i], block_of(before, 0, KS[i]), at_y(1))
        up_fm[i].wait_recv()
        got["u", 1, i] = wire.send(fm_ref.at[i], block_of(after, 64, KS[i]), at_y(3))
        if i + WINDOW < 8:
            up_first(i + WINDOW)

    def up_share(i):
        for side in range(2):
            got["u", side, i].wait_recv()
            block = block_of(across, side * 64, KS[i])
            got["us", side, i] = wire.send(block, block, mate)

    def up_end(i):
        if i == 0:
            to_mate.wait_recv()
        for side in range(2):
            got["us", side, i].wait_recv()

    def prepare():
        lane = lax.broadcasted_iota(jnp.int32, (ROWS, BLOCK), 1)
        spot = jnp.where(lane < 64, lane, lane - 64)
        seg = jnp.broadcast_to(seg_ref[...].astype(F32), (BLOCK, ROWS)).T
        same = seg == spot.astype(F32)
        qaug_ref[...] = jnp.where(same, 1.0, 0.0).astype(BF16)
        kaug_ref[...] = jnp.where((spot < 3) & jnp.logical_not(same), FAR, 0.0).astype(BF16)
        oh_ref[...] = jnp.where(
            lax.broadcasted_iota(jnp.int32, (32, WIDE), 0) == bucket_ref[...], 1.0, 0.0
        )
        bext_ref[...] = jnp.dot(
            table_ref[...], oh_ref[...], precision=lax.Precision.HIGHEST, preferred_element_type=F32
        )
        pb_ref[...] = jnp.zeros_like(pb_ref)
        dsb_ref[...] = jnp.zeros_like(dsb_ref)

    def columns(p):
        return pl.ds(p * BLOCK, BLOCK)

    def own_lanes(odd):
        lane = lax.broadcasted_iota(jnp.int32, (ROWS, BLOCK), 1)
        return (lane >= 64) if odd else (lane < 64)

    def softmax_head(h):
        p, odd = h // 2, h % 2
        qp, kp = q_ref[:, columns(p)], k_ref[:, columns(p)]
        if True:
            own = own_lanes(odd)
            q_h = jnp.where(own, qp, qaug_ref[...])
            k_h = jnp.where(own, kp, kaug_ref[...])
            bias = bext_ref[pl.ds(h, 1), :]
            for d in range(5):
                strip = jnp.broadcast_to(bias[:, d * BLOCK : (d + 2) * BLOCK], (BLOCK, 2 * BLOCK))
                toe_ref[d] = pltpu.roll(strip, 0, 1, stride=1, stride_axis=0)[:, BLOCK:]
            for i2 in range(2):
                peak = [None, None]
                for j in range(4):
                    s2 = nt(k_h[j * BLOCK : (j + 1) * BLOCK], q_h[i2 * 256 : (i2 + 1) * 256])
                    for sub in range(2):
                        i = 2 * i2 + sub
                        if abs(i - j) <= 2:
                            s = s2[:, sub * BLOCK : (sub + 1) * BLOCK] + toe_ref[i - j + 2]
                            e_ref[h, j * BLOCK : (j + 1) * BLOCK, i * BLOCK : (i + 1) * BLOCK] = s
                            top = jnp.max(s.reshape(16, 8, BLOCK), axis=0)
                            peak[sub] = top if peak[sub] is None else jnp.maximum(peak[sub], top)
                for sub in range(2):
                    i = 2 * i2 + sub
                    top = jnp.max(peak[sub], axis=0, keepdims=True)
                    total = None
                    for j in range(4):
                        if abs(i - j) <= 2:
                            at = (h, slice(j * BLOCK, (j + 1) * BLOCK), slice(i * BLOCK, (i + 1) * BLOCK))
                            e = jnp.exp(e_ref[at] - top)
                            e_ref[at] = e
                            part = jnp.sum(e.reshape(16, 8, BLOCK), axis=0)
                            total = part if total is None else total + part
                    r_ref[pl.ds(h, 1), i * BLOCK : (i + 1) * BLOCK] = 1.0 / jnp.sum(
                        total, axis=0, keepdims=True
                    )

    def context(which, m):
        w = (wa_ref if which == 0 else wb_ref)[...].reshape(D, HALF)
        rows = slice(m * 256, (m + 1) * 256)
        ctx_ref[rows, which * HALF : (which + 1) * HALF] = nn(g_ref[rows, :], w).astype(BF16)

    def backward_head(h):
        p, odd = h // 2, h % 2
        qp, kp = q_ref[:, columns(p)], k_ref[:, columns(p)]
        vp, gp = v_ref[:, columns(p)], ctx_ref[:, columns(p)]
        kpt = kp.T
        if True:
            own = own_lanes(odd)
            g_h = jnp.where(own, gp, jnp.zeros_like(gp))
            delta = []
            for i2 in range(2):
                sums = [None, None]
                for j in range(4):
                    d2 = nt(vp[j * BLOCK : (j + 1) * BLOCK], g_h[i2 * 256 : (i2 + 1) * 256])
                    for sub in range(2):
                        i = 2 * i2 + sub
                        if abs(i - j) <= 2:
                            js, cs = slice(j * BLOCK, (j + 1) * BLOCK), slice(i * BLOCK, (i + 1) * BLOCK)
                            d1 = d2[:, sub * BLOCK : (sub + 1) * BLOCK]
                            dp_ref[js, cs] = d1
                            part = jnp.sum((e_ref[h, js, cs] * d1).reshape(16, 8, BLOCK), axis=0)
                            sums[sub] = part if sums[sub] is None else sums[sub] + part
                for sub in range(2):
                    i = 2 * i2 + sub
                    recip = r_ref[pl.ds(h, 1), i * BLOCK : (i + 1) * BLOCK]
                    delta.append(recip * jnp.sum(sums[sub], axis=0, keepdims=True))
            g8_ref[...] = jnp.zeros_like(g8_ref)
            for d in range(-2, 3):
                diag = None
                for j in range(4):
                    i = j + d
                    if 0 <= i < 4:
                        js, cs = slice(j * BLOCK, (j + 1) * BLOCK), slice(i * BLOCK, (i + 1) * BLOCK)
                        probs = e_ref[h, js, cs] * r_ref[pl.ds(h, 1), cs]
                        ds = probs * (dp_ref[js, cs] - delta[i])
                        pb_ref[js, cs] = probs.astype(BF16)
                        dsb_ref[js, cs] = ds.astype(BF16)
                        diag = ds if diag is None else diag + ds
                strip = jnp.concatenate([jnp.zeros_like(diag), diag], axis=1)
                total = strip[0:8]
                for g in range(1, 16):
                    total = total + pltpu.roll(strip[8 * g : 8 * g + 8], 2 * BLOCK - 8 * g, 1)
                cs = slice((d + 2) * BLOCK, (d + 4) * BLOCK)
                g8_ref[:, cs] = g8_ref[:, cs] + total
            row = g8_ref[0:1, :]
            for s in range(1, 8):
                row = row + pltpu.roll(g8_ref[s : s + 1, :], WIDE - s, 1)
            gb_ref[pl.ds(h, 1), :] = row
            side = slice(64 * odd, 64 * odd + 64)
            dqt_ref[side, :] = nn(kpt[side, :], dsb_ref[...])
            dk_h, dv_h = nn(dsb_ref[...], qp), nn(pb_ref[...], gp)
            if odd == 0:
                dkp_ref[...] = dk_h
                dvp_ref[...] = dv_h
            else:
                dk_ref[:, columns(p)] = jnp.where(own, dk_h, dkp_ref[...]).astype(BF16)
                dv_ref[:, columns(p)] = jnp.where(own, dv_h, dvp_ref[...]).astype(BF16)
        if odd == 1:
            dq_ref[:, columns(p)] = dqt_ref[...].T.astype(BF16)

    def term(k):
        z_at = zs(k)
        block = lax.dot_general(
            g_ref[:, pl.ds(pl.multiple_of(z_at * 512, 512), 512)],
            att_ref[...],
            (((0,), (0,)), ((), ())),
            preferred_element_type=F32,
        ).astype(BF16)
        ta_ref[z_at] = block[:, :BLOCK].reshape(2, 4, 64, BLOCK)
        tc_ref[z_at] = block[:, BLOCK:HALF].reshape(2, 4, 64, BLOCK)
        tb_ref[z_at] = block[:, HALF:].reshape(2, 4, 64, HALF)

    def total(*parts):
        out = parts[0].astype(F32)
        for part in parts[1:]:
            out = out + part.astype(F32)
        return out

    def sum_a_hop(k, way, part):
        come = rap_ref if way == 1 else ram_ref
        z_at = zs(k if way == 1 else 8 - k)
        if ("sa", k, way, part) in got:
            got["sa", k, way, part].wait_recv()
            ta_ref[z_at, part] = total(ta_ref[z_at, part], come[k, part]).astype(BF16)
        got["sa", k - 1, way, part] = wire.send(
            ta_ref.at[z_at, part], come.at[k - 1, part], z_next(way)
        )

    def sum_a_step(k):
        for part in range(2):
            for way in (1, -1):
                sum_a_hop(k, way, part)

    def sum_a_x(part):
        for way in (1, -1):
            got["sa", 0, way, part].wait_recv()
        full = total(ta_ref[z, part], rap_ref[0, part], ram_ref[0, part])
        saf_ref[part] = full
        sa_ref[part] = full.astype(BF16)
        for k in (2, 1, 3):
            got["sax", part, k] = wire.send(sa_ref.at[part, xs(k)], rax_ref.at[part, k - 1], at_x(k))

    def sum_a_y():
        for part in range(2):
            full = saf_ref[part, x]
            for k in (1, 3, 2):
                got["sax", part, k].wait_recv()
                full = full + rax_ref[part, k - 1].astype(F32)
            saf_ref[part, x] = full
            say_ref[part] = full.astype(BF16)
        got["say"] = wire.send(say_ref.at[1 - yl], ray_ref, pair)

    def sum_a_end():
        got["say"].wait_recv()
        wg_ref[:, :BLOCK] = total(saf_ref[yl, x], ray_ref[...])

    def sum_c_y(k):
        got["scy", k] = wire.send(tc_ref.at[zs(k), 1 - yl], rcy_ref.at[k], pair)

    def sum_c_hop(k, way):
        come = rcp_ref if way == 1 else rcm_ref
        rel = k if way == 1 else 8 - k
        got["scy", rel].wait_recv()
        parts = [tc_ref[zs(rel), yl], rcy_ref[rel]]
        if ("sc", k, way) in got:
            got["sc", k, way].wait_recv()
            parts.append(come[k])
        tc_ref[zs(rel), yl] = total(*parts).astype(BF16)
        got["sc", k - 1, way] = wire.send(tc_ref.at[zs(rel), yl], come.at[k - 1], z_next(way))

    def sum_c_step(k):
        for way in (1, -1):
            sum_c_hop(k, way)

    def sum_c_x():
        got["scy", 0].wait_recv()
        for way in (1, -1):
            got["sc", 0, way].wait_recv()
        full = total(tc_ref[z, yl], rcy_ref[0], rcp_ref[0], rcm_ref[0])
        scf_ref[...] = full
        sc_ref[...] = full.astype(BF16)
        for k in (2, 1, 3):
            got["scx", k] = wire.send(sc_ref.at[xs(k)], rcx_ref.at[k - 1], at_x(k))

    def sum_c_end():
        full = scf_ref[x]
        for k in (1, 3, 2):
            got["scx", k].wait_recv()
            full = full + rcx_ref[k - 1].astype(F32)
        wg_ref[:, BLOCK:HALF] = full

    def sum_b_first(k, side):
        other = 4 - side
        come = rbp_ref if side == 1 else rbm_ref
        back = rbm_ref if side == 1 else rbp_ref
        got["sb2", k] = wire.send(tb_ref.at[zs(k), :, xs(2)], come.at[k, 1], at_x(side))
        got["sb1", k, other] = wire.send(tb_ref.at[zs(k), :, xs(other)], back.at[k, 0], at_x(other))

    def sum_b_second(k, side):
        come = rbp_ref if side == 1 else rbm_ref
        got["sb2", k].wait_recv()
        at = (zs(k), slice(None), xs(side))
        tb_ref[at] = total(tb_ref[at], come[k, 1]).astype(BF16)
        got["sb1", k, side] = wire.send(tb_ref.at[at], come.at[k, 0], at_x(side))

    def sum_b_y(k):
        for side in (1, 3):
            got["sb1", k, side].wait_recv()
        full = total(tb_ref[zs(k), :, x], rbp_ref[k, 0], rbm_ref[k, 0])
        sbf_ref[k] = full
        sby_ref[k] = full.astype(BF16)
        got["sby", k] = wire.send(sby_ref.at[k, 1 - yl], rby_ref.at[k], pair)

    def sum_b_z(k):
        got["sby", k].wait_recv()
        full = total(sbf_ref[k, yl], rby_ref[k])
        if k:
            sbz_ref[k] = full.astype(BF16)
            got["sbz", k] = wire.send(sbz_ref.at[k], rbz_ref.at[k - 1], at_z(k))
        else:
            sbf_ref[0, 0] = full

    def sum_b_end():
        full = sbf_ref[0, 0]
        for k in range(1, 8):
            got["sbz", k].wait_recv()
            full = full + rbz_ref[k - 1].astype(F32)
        wg_ref[:, HALF:] = full

    def table_z():
        here = lax.dot_general(
            gb_ref[...], oh_ref[...], (((1,), (1,)), ((), ())),
            precision=lax.Precision.HIGHEST, preferred_element_type=F32,
        )
        tz_ref[...] = jnp.concatenate([here, jnp.zeros((HEADS, BLOCK - 32), F32)], axis=1)
        for k in range(1, 8):
            got["tz", k] = wire.send(tz_ref, rtz_ref.at[k - 1], at_z(k))

    def table_xy():
        full = tz_ref[...]
        for k in range(1, 8):
            got["tz", k].wait_recv()
            full = full + rtz_ref[k - 1]
        tx_ref[...] = full
        for k, device in enumerate(around):
            got["tx", k] = wire.send(tx_ref, rtx_ref.at[k], device)

    def table_end():
        full = tx_ref[...]
        for k in range(7):
            got["tx", k].wait_recv()
            full = full + rtx_ref[k]
        tg_ref[...] = full[:, :32]

    def sums_start(i):
        k = KS[i]
        term(k)
        if k == 4:
            sum_a_hop(4, 1, 0)
            sum_a_hop(4, -1, 1)
        if k == 3:
            sum_a_hop(3, 1, 1)
        if k == 5:
            sum_a_hop(3, -1, 0)
        sum_c_y(k)
        sum_b_first(k, 1 if i % 2 == 0 else 3)

    prepare()
    gather_first()
    up_hand_on(0)
    softmax_head(0)
    up_hand_on(1)
    gather_b_step(1)
    gather_a_start()
    up_hand_on(2)
    softmax_head(1)
    gather_b_across(0)
    up_share(0)
    gather_b_step(2)

    up_end(0)
    sums_start(0)
    up_hand_on(3)
    up_share(1)
    gather_b_across(1)
    gather_b_across(7)
    softmax_head(2)
    up_end(1)
    sums_start(1)
    up_hand_on(4)
    up_share(2)
    gather_a_step(1)
    softmax_head(3)
    up_end(2)
    sums_start(2)
    up_hand_on(5)
    up_share(3)
    gather_b_step(3)
    gather_b_across(2)
    gather_b_across(6)
    softmax_head(4)
    up_end(3)
    sums_start(3)
    up_hand_on(6)
    up_share(4)
    sum_a_hop(3, 1, 0)
    sum_a_hop(3, -1, 1)
    sum_c_hop(4, 1)
    gather_a_step(2)
    softmax_head(5)
    up_end(4)
    sums_start(4)
    up_hand_on(7)
    up_share(5)
    gather_b_step(4)
    gather_b_across(3)
    gather_b_across(5)
    sum_b_second(4, 1)
    sum_b_second(3, 3)
    softmax_head(6)
    up_end(5)
    sums_start(5)
    up_share(6)
    sum_a_step(2)
    sum_c_step(3)
    gather_a_step(3)
    softmax_head(7)
    up_end(6)
    sums_start(6)
    up_share(7)
    gather_b_across(4)
    sum_b_second(5, 1)
    sum_b_second(2, 3)
    sum_b_y(4)
    sum_b_y(3)
    up_end(7)
    sums_start(7)
    sum_a_step(1)
    sum_c_step(2)
    sum_b_second(6, 1)
    sum_b_second(1, 3)
    gather_a_end()
    context(0, 0)
    context(0, 1)
    gather_b_end()
    context(1, 0)
    context(1, 1)
    backward_head(0)
    sum_b_second(7, 1)
    sum_b_second(0, 3)
    backward_head(1)
    sum_c_step(1)
    backward_head(2)
    sum_b_y(5)
    sum_b_y(2)
    sum_b_z(4)
    sum_b_z(3)
    backward_head(3)
    sum_a_x(0)
    sum_a_x(1)
    backward_head(4)
    sum_b_y(6)
    sum_b_y(1)
    sum_b_z(5)
    sum_b_z(2)
    backward_head(5)
    sum_c_x()
    sum_a_y()
    backward_head(6)
    sum_b_y(7)
    sum_b_y(0)
    backward_head(7)
    table_z()
    sum_b_z(6)
    sum_b_z(1)
    sum_b_z(7)
    sum_b_z(0)
    sum_c_end()
    table_xy()
    sum_a_end()
    sum_b_end()
    table_end()
    wire.finish()


def carry(*refs):
    for src, dst in zip(refs[:5], refs[5:]):
        dst[...] = src[...]


def on_device(queries, keys, values, attended, upstream, out_weight, bias_table, buckets, segments):
    shifted = jnp.pad(buckets, (129, WIDE - 129 - buckets.shape[0]), constant_values=-1)[None, :]
    anywhere = pl.BlockSpec(memory_space=pl.ANY)
    inside = pl.BlockSpec(memory_space=pltpu.VMEM)
    bf, f4 = (lambda *s: pltpu.VMEM(s, BF16)), (lambda *s: pltpu.VMEM(s, F32))
    shapes = (
        jax.ShapeDtypeStruct((ROWS, FEAT), BF16),
        jax.ShapeDtypeStruct((ROWS, FEAT), BF16),
        jax.ShapeDtypeStruct((ROWS, FEAT), BF16),
        jax.ShapeDtypeStruct((64, FEAT), F32),
        jax.ShapeDtypeStruct((HEADS, 32), F32),
    )
    made = pl.pallas_call(
        kernel,
        out_shape=shapes,
        in_specs=[anywhere] * 6 + [inside] * 3,
        out_specs=(inside,) * 5,
        scratch_shapes=[
            bf(ROWS, FEAT), bf(ROWS, FEAT), bf(ROWS, FEAT), bf(ROWS, FEAT),
            bf(ROWS, D), bf(ROWS, FEAT),
            bf(8, 2, 4, 64, HALF), bf(8, 2, 4, 64, HALF),
            bf(8, 64, FEAT), bf(8, 64, FEAT),
            bf(8, 2, 4, 64, BLOCK), bf(8, 2, 4, 64, BLOCK), bf(8, 2, 4, 64, HALF),
            bf(4, 2, 4, 64, BLOCK), bf(4, 2, 4, 64, BLOCK), bf(2, 4, 64, BLOCK), f4(2, 4, 64, BLOCK),
            bf(2, 3, 64, BLOCK), bf(64, BLOCK), bf(2, 64, BLOCK),
            bf(8, 4, 64, BLOCK), bf(4, 4, 64, BLOCK), bf(4, 4, 64, BLOCK), bf(4, 64, BLOCK),
            f4(4, 64, BLOCK), bf(3, 64, BLOCK),
            bf(8, 2, 2, 64, HALF), bf(8, 2, 2, 64, HALF), bf(8, 2, 64, HALF), f4(8, 2, 64, HALF),
            bf(8, 64, HALF), bf(8, 64, HALF), bf(7, 64, HALF),
            f4(HEADS, ROWS, ROWS), f4(HEADS, ROWS), f4(ROWS, ROWS), bf(ROWS, ROWS), bf(ROWS, ROWS),
            f4(5, BLOCK, BLOCK), f4(HEADS, WIDE), f4(32, WIDE), f4(HEADS, WIDE), f4(8, WIDE),
            bf(ROWS, BLOCK), bf(ROWS, BLOCK), f4(BLOCK, ROWS), f4(ROWS, BLOCK), f4(ROWS, BLOCK),
            f4(HEADS, BLOCK), f4(7, HEADS, BLOCK), f4(HEADS, BLOCK), f4(7, HEADS, BLOCK),
            pltpu.SemaphoreType.DMA((7,)),
            pltpu.SemaphoreType.DMA((N_SEM,)),
            pltpu.SemaphoreType.DMA((N_SEM,)),
        ],
        compiler_params=pltpu.CompilerParams(
            collective_id=0, has_side_effects=True, vmem_limit_bytes=60 * 1024 * 1024
        ),
    )(
        queries, keys, values, attended, upstream, out_weight.T, bias_table.T, shifted, segments[None, :]
    )
    dq, dk, dv, wg, tg = pl.pallas_call(
        carry,
        out_shape=shapes,
        in_specs=[inside] * 5,
        out_specs=(inside,) * 5,
    )(*made)
    return dq, dk, dv, wg, tg.T


def solution(mesh):
    in_specs = (
        P("dp", "tensor"),
        P("dp", "tensor"),
        P("dp", "tensor"),
        P("dp", "tensor"),
        P(("dp", "tensor"), None),
        P("tensor", "dp"),
        P(None, "tensor"),
        P(),
        P("dp"),
    )
    out_specs = (
        P("dp", "tensor"),
        P("dp", "tensor"),
        P("dp", "tensor"),
        P("dp", "tensor"),
        P(None, "tensor"),
    )
    return jax.shard_map(
        on_device, mesh=mesh, in_specs=in_specs, out_specs=out_specs, check_vma=False
    )
```

```python
import jax
import jax.numpy as jnp
from jax import lax
from jax.experimental import pallas as pl
from jax.experimental.pallas import tpu as pltpu
from jax.sharding import PartitionSpec as P

MESH = pl.DeviceIdType.MESH
F32 = jnp.float32
BF16 = jnp.bfloat16
ROWS = 512
FEAT = 512
HALF = 256
D = 4096
HEADS = 8
WIDE = 768
BLOCK = 128
FAR = -4096.0
N_SEM = 224
KS = (4, 3, 5, 2, 6, 1, 7, 0)
WINDOW = 3


def nt(a, b):
    return lax.dot_general(a, b, (((1,), (1,)), ((), ())), preferred_element_type=F32)


def nn(a, b):
    return jnp.dot(a, b, preferred_element_type=F32)


class Wire:
    def __init__(self, send_sem, recv_sem):
        self.send_sem, self.recv_sem = send_sem, recv_sem
        self.made = []

    def send(self, src, dst, device):
        at = len(self.made)
        copy = pltpu.make_async_remote_copy(
            src_ref=src,
            dst_ref=dst,
            send_sem=self.send_sem.at[at],
            recv_sem=self.recv_sem.at[at],
            device_id=device,
            device_id_type=MESH,
        )
        copy.start()
        self.made.append(copy)
        return copy

    def finish(self):
        for copy in self.made:
            copy.wait_send()


def kernel(
    q_hbm, k_hbm, v_hbm, att_hbm, up_hbm, wt_hbm, table_ref, bucket_ref, seg_ref,
    dq_ref, dk_ref, dv_ref, wg_ref, tg_ref,
    q_ref, k_ref, v_ref, att_ref, g_ref, ctx_ref, wa_ref, wb_ref, fp_ref, fm_ref,
    ta_ref, tc_ref, tb_ref,
    rap_ref, ram_ref, sa_ref, saf_ref, rax_ref, ray_ref, say_ref,
    rcy_ref, rcp_ref, rcm_ref, sc_ref, scf_ref, rcx_ref,
    rbp_ref, rbm_ref, sby_ref, sbf_ref, rby_ref, sbz_ref, rbz_ref,
    e_ref, r_ref, dp_ref, pb_ref, dsb_ref, toe_ref, bext_ref, oh_ref, gb_ref, g8_ref,
    qaug_ref, kaug_ref, dqt_ref, dkp_ref, dvp_ref,
    tz_ref, rtz_ref, tx_ref, rtx_ref,
    local_sem, send_sem, recv_sem,
):
    me, tensor = lax.axis_index("dp"), lax.axis_index("tensor")
    x, yl, z = lax.rem(me, 4), lax.rem(lax.div(me, 4), 2), lax.div(me, 8)
    core, yh = lax.rem(tensor, 2), lax.div(tensor, 2)
    y = yh * 2 + yl

    def place(z_at, yl_at, x_at, yh_at, core_at):
        return {"dp": z_at * 8 + yl_at * 4 + x_at, "tensor": yh_at * 2 + core_at}

    def xs(k):
        return lax.rem(x + k, 4)

    def zs(k):
        return lax.rem(z + k, 8)

    def at_x(k):
        return place(z, yl, xs(k), yh, core)

    def at_z(k):
        return place(zs(k), yl, x, yh, core)

    def at_y(k):
        there = lax.rem(y + k, 4)
        return place(z, lax.rem(there, 2), x, lax.div(there, 2), core)

    pair = place(z, 1 - yl, x, yh, core)
    mate = place(z, yl, x, yh, 1 - core)

    loads = []
    for at, (src, dst) in enumerate(
        [
            (q_hbm, q_ref),
            (k_hbm, k_ref),
            (v_hbm, v_ref),
            (att_hbm, att_ref),
            (up_hbm, g_ref.at[pl.ds(pl.multiple_of(tensor * 128, 128), 128), :]),
            (wt_hbm.at[:, pl.ds(0, HALF)], wa_ref.at[z, yl, x]),
            (wt_hbm.at[:, pl.ds(HALF, HALF)], wb_ref.at[z, yl, x]),
        ]
    ):
        copy = pltpu.make_async_copy(src, dst, local_sem.at[at])
        copy.start()
        loads.append(copy)

    barrier = pltpu.get_barrier_semaphore()
    around = [at_x(k) for k in range(1, 4)] + [place(z, 1 - yl, xs(k), yh, core) for k in range(4)]
    greeted = [at_z(k) for k in range(1, 8)] + around + [place(z, 1 - yl, x, 1 - yh, core), mate]
    for device in greeted:
        pl.semaphore_signal(barrier, inc=1, device_id=device, device_id_type=MESH)
    pl.semaphore_wait(barrier, len(greeted))

    wire = Wire(send_sem, recv_sem)
    got = {}

    y_a = wire.send(wt_hbm.at[:, pl.ds(0, HALF)], wa_ref.at[z, yl, x], pair)
    y_b = wire.send(wt_hbm.at[:, pl.ds(HALF, HALF)], wb_ref.at[z, yl, x], pair)
    up_fp, up_fm = {}, {}

    def cols(k):
        return pl.ds(pl.multiple_of(zs(k) * FEAT, FEAT), FEAT)

    def up_first(i):
        up_fp[i] = wire.send(up_hbm.at[pl.ds(0, 64), cols(KS[i])], fp_ref.at[i], at_y(1))
        up_fm[i] = wire.send(up_hbm.at[pl.ds(64, 64), cols(KS[i])], fm_ref.at[i], at_y(3))

    for i in range(WINDOW):
        up_first(i)
    own_rows = pl.multiple_of(tensor * 128, 128)
    to_mate = wire.send(up_hbm, g_ref.at[pl.ds(own_rows, 128), :], mate)
    for copy in loads:
        copy.wait()

    before = lax.div(lax.rem(y + 3, 4), 2) * 2 + core
    after = lax.div(lax.rem(y + 1, 4), 2) * 2 + core
    across = (1 - yh) * 2 + core

    def gather_first():
        y_a.wait_recv()
        y_b.wait_recv()
        got["a_x"] = [wire.send(wa_ref.at[z, :, x], wa_ref.at[z, :, x], at_x(k)) for k in (1, 3, 2)]
        for way in (1, -1):
            got["b_z", 1, way] = b_hop(1, way)
            got["a_z", 1, way, 0] = a_hop(1, way, 0)
        b_spread(0)

    def far(step, way):
        return zs(8 - step if way == 1 else step)

    def z_next(way):
        return at_z(1 if way == 1 else 7)

    def a_hop(step, way, part):
        chunk = wa_ref.at[far(step - 1, way), :, xs(part)]
        return wire.send(chunk, chunk, z_next(way))

    def gather_a_start():
        for copy, part in zip(got["a_x"], (3, 1, 2)):
            copy.wait_recv()
            for way in (1, -1):
                got["a_z", 1, way, part] = a_hop(1, way, part)

    def gather_a_step(step):
        for part in (0, 3, 1, 2):
            for way in (1, -1):
                got["a_z", step, way, part].wait_recv()
                if step < 3 or (part in (0, 3)) == (way == 1):
                    got["a_z", step + 1, way, part] = a_hop(step + 1, way, part)

    def gather_a_end():
        for part, way in ((0, 1), (3, 1), (1, -1), (2, -1)):
            got["a_z", 4, way, part].wait_recv()

    def b_hop(step, way):
        chunk = wb_ref.at[far(step - 1, way), :, x]
        return wire.send(chunk, chunk, z_next(way))

    def b_half_hop(way):
        chunk = wb_ref.at[far(3, way), 0 if way == 1 else 1, x]
        return wire.send(chunk, chunk, z_next(way))

    def b_spread(k):
        chunk = wb_ref.at[zs(k), :, x]
        for side in (1, 3):
            got["b_x", k, side] = wire.send(chunk, chunk, at_x(side))

    def gather_b_step(step):
        for way in (1, -1):
            if step < 4:
                got["b_z", step, way].wait_recv()
            else:
                got["b_z", 4, way].wait_recv()
            if step < 3:
                got["b_z", step + 1, way] = b_hop(step + 1, way)
            elif step == 3:
                got["b_z", 4, way] = b_half_hop(way)
            if step < 4:
                b_spread(8 - step if way == 1 else step)
        if step == 4:
            b_spread(4)

    def gather_b_across(k):
        for side in (1, 3):
            got["b_x", k, side].wait_recv()
            chunk = wb_ref.at[zs(k), 0 if side == 1 else 1, xs(3 if side == 1 else 1)]
            got["b_x2", k, side] = wire.send(chunk, chunk, at_x(side))

    def gather_b_end():
        for k in range(8):
            for side in (1, 3):
                got["b_x2", k, side].wait_recv()

    def block_of(owner, first, k):
        return g_ref.at[pl.ds(pl.multiple_of(owner * 128 + first, 64), 64), cols(k)]

    def up_hand_on(i):
        up_fp[i].wait_recv()
        got["u", 0, i] = wire.send(fp_ref.at[i], block_of(before, 0, KS[i]), at_y(1))
        up_fm[i].wait_recv()
        got["u", 1, i] = wire.send(fm_ref.at[i], block_of(after, 64, KS[i]), at_y(3))
        if i + WINDOW < 8:
            up_first(i + WINDOW)

    def up_share(i):
        for side in range(2):
            got["u", side, i].wait_recv()
            block = block_of(across, side * 64, KS[i])
            got["us", side, i] = wire.send(block, block, mate)

    def up_end(i):
        if i == 0:
            to_mate.wait_recv()
        for side in range(2):
            got["us", side, i].wait_recv()

    def prepare():
        lane = lax.broadcasted_iota(jnp.int32, (ROWS, BLOCK), 1)
        spot = jnp.where(lane < 64, lane, lane - 64)
        seg = jnp.broadcast_to(seg_ref[...].astype(F32), (BLOCK, ROWS)).T
        same = seg == spot.astype(F32)
        qaug_ref[...] = jnp.where(same, 1.0, 0.0).astype(BF16)
        kaug_ref[...] = jnp.where((spot < 3) & jnp.logical_not(same), FAR, 0.0).astype(BF16)
        oh_ref[...] = jnp.zeros_like(oh_ref)
        oh_ref[:, BLOCK + 1 : BLOCK + 512] = jnp.where(
            lax.broadcasted_iota(jnp.int32, (32, 511), 0) == bucket_ref[...], 1.0, 0.0
        )
        bext_ref[...] = jnp.dot(
            table_ref[...], oh_ref[...], precision=lax.Precision.HIGHEST, preferred_element_type=F32
        )
        pb_ref[...] = jnp.zeros_like(pb_ref)
        dsb_ref[...] = jnp.zeros_like(dsb_ref)

    def columns(p):
        return pl.ds(p * BLOCK, BLOCK)

    def own_lanes(odd):
        lane = lax.broadcasted_iota(jnp.int32, (ROWS, BLOCK), 1)
        return (lane >= 64) if odd else (lane < 64)

    def softmax_head(h):
        p, odd = h // 2, h % 2
        qp, kp = q_ref[:, columns(p)], k_ref[:, columns(p)]
        if True:
            own = own_lanes(odd)
            q_h = jnp.where(own, qp, qaug_ref[...])
            k_h = jnp.where(own, kp, kaug_ref[...])
            bias = bext_ref[pl.ds(h, 1), :]
            for d in range(5):
                strip = jnp.broadcast_to(bias[:, d * BLOCK : (d + 2) * BLOCK], (BLOCK, 2 * BLOCK))
                toe_ref[d] = pltpu.roll(strip, 0, 1, stride=1, stride_axis=0)[:, BLOCK:]
            for i2 in range(2):
                peak = [None, None]
                for j in range(4):
                    s2 = nt(k_h[j * BLOCK : (j + 1) * BLOCK], q_h[i2 * 256 : (i2 + 1) * 256])
                    for sub in range(2):
                        i = 2 * i2 + sub
                        if abs(i - j) <= 2:
                            s = s2[:, sub * BLOCK : (sub + 1) * BLOCK] + toe_ref[i - j + 2]
                            e_ref[h, j * BLOCK : (j + 1) * BLOCK, i * BLOCK : (i + 1) * BLOCK] = s
                            top = jnp.max(s.reshape(16, 8, BLOCK), axis=0)
                            peak[sub] = top if peak[sub] is None else jnp.maximum(peak[sub], top)
                for sub in range(2):
                    i = 2 * i2 + sub
                    top = jnp.max(peak[sub], axis=0, keepdims=True)
                    total = None
                    for j in range(4):
                        if abs(i - j) <= 2:
                            at = (h, slice(j * BLOCK, (j + 1) * BLOCK), slice(i * BLOCK, (i + 1) * BLOCK))
                            e = jnp.exp(e_ref[at] - top)
                            e_ref[at] = e
                            part = jnp.sum(e.reshape(16, 8, BLOCK), axis=0)
                            total = part if total is None else total + part
                    r_ref[pl.ds(h, 1), i * BLOCK : (i + 1) * BLOCK] = 1.0 / jnp.sum(
                        total, axis=0, keepdims=True
                    )

    def context(which, m):
        w = (wa_ref if which == 0 else wb_ref)[...].reshape(D, HALF)
        rows = slice(m * 256, (m + 1) * 256)
        ctx_ref[rows, which * HALF : (which + 1) * HALF] = nn(g_ref[rows, :], w).astype(BF16)

    def backward_head(h):
        p, odd = h // 2, h % 2
        qp, kp = q_ref[:, columns(p)], k_ref[:, columns(p)]
        vp, gp = v_ref[:, columns(p)], ctx_ref[:, columns(p)]
        kpt = kp.T
        if True:
            own = own_lanes(odd)
            g_h = jnp.where(own, gp, jnp.zeros_like(gp))
            delta = []
            for i2 in range(2):
                sums = [None, None]
                for j in range(4):
                    d2 = nt(vp[j * BLOCK : (j + 1) * BLOCK], g_h[i2 * 256 : (i2 + 1) * 256])
                    for sub in range(2):
                        i = 2 * i2 + sub
                        if abs(i - j) <= 2:
                            js, cs = slice(j * BLOCK, (j + 1) * BLOCK), slice(i * BLOCK, (i + 1) * BLOCK)
                            d1 = d2[:, sub * BLOCK : (sub + 1) * BLOCK]
                            dp_ref[js, cs] = d1
                            part = jnp.sum((e_ref[h, js, cs] * d1).reshape(16, 8, BLOCK), axis=0)
                            sums[sub] = part if sums[sub] is None else sums[sub] + part
                for sub in range(2):
                    i = 2 * i2 + sub
                    recip = r_ref[pl.ds(h, 1), i * BLOCK : (i + 1) * BLOCK]
                    delta.append(recip * jnp.sum(sums[sub], axis=0, keepdims=True))
            g8_ref[...] = jnp.zeros_like(g8_ref)
            for d in range(-2, 3):
                diag = None
                for j in range(4):
                    i = j + d
                    if 0 <= i < 4:
                        js, cs = slice(j * BLOCK, (j + 1) * BLOCK), slice(i * BLOCK, (i + 1) * BLOCK)
                        probs = e_ref[h, js, cs] * r_ref[pl.ds(h, 1), cs]
                        ds = probs * (dp_ref[js, cs] - delta[i])
                        pb_ref[js, cs] = probs.astype(BF16)
                        dsb_ref[js, cs] = ds.astype(BF16)
                        diag = ds if diag is None else diag + ds
                strip = jnp.concatenate([jnp.zeros_like(diag), diag], axis=1)
                total = strip[0:8]
                for g in range(1, 16):
                    total = total + pltpu.roll(strip[8 * g : 8 * g + 8], 2 * BLOCK - 8 * g, 1)
                cs = slice((d + 2) * BLOCK, (d + 4) * BLOCK)
                g8_ref[:, cs] = g8_ref[:, cs] + total
            row = g8_ref[0:1, :]
            for s in range(1, 8):
                row = row + pltpu.roll(g8_ref[s : s + 1, :], WIDE - s, 1)
            gb_ref[pl.ds(h, 1), :] = row
            side = slice(64 * odd, 64 * odd + 64)
            dqt_ref[side, :] = nn(kpt[side, :], dsb_ref[...])
            dk_h, dv_h = nn(dsb_ref[...], qp), nn(pb_ref[...], gp)
            if odd == 0:
                dkp_ref[...] = dk_h
                dvp_ref[...] = dv_h
            else:
                dk_ref[:, columns(p)] = jnp.where(own, dk_h, dkp_ref[...]).astype(BF16)
                dv_ref[:, columns(p)] = jnp.where(own, dv_h, dvp_ref[...]).astype(BF16)
        if odd == 1:
            dq_ref[:, columns(p)] = dqt_ref[...].T.astype(BF16)

    def term(k):
        z_at = zs(k)
        block = lax.dot_general(
            g_ref[:, pl.ds(pl.multiple_of(z_at * 512, 512), 512)],
            att_ref[...],
            (((0,), (0,)), ((), ())),
            preferred_element_type=F32,
        ).astype(BF16)
        ta_ref[z_at] = block[:, :BLOCK].reshape(2, 4, 64, BLOCK)
        tc_ref[z_at] = block[:, BLOCK:HALF].reshape(2, 4, 64, BLOCK)
        tb_ref[z_at] = block[:, HALF:].reshape(2, 4, 64, HALF)

    def total(*parts):
        out = parts[0].astype(F32)
        for part in parts[1:]:
            out = out + part.astype(F32)
        return out

    def sum_a_hop(k, way, part):
        come = rap_ref if way == 1 else ram_ref
        z_at = zs(k if way == 1 else 8 - k)
        if ("sa", k, way, part) in got:
            got["sa", k, way, part].wait_recv()
            ta_ref[z_at, part] = total(ta_ref[z_at, part], come[k, part]).astype(BF16)
        got["sa", k - 1, way, part] = wire.send(
            ta_ref.at[z_at, part], come.at[k - 1, part], z_next(way)
        )

    def sum_a_step(k):
        for part in range(2):
            for way in (1, -1):
                sum_a_hop(k, way, part)

    def sum_a_x(part):
        for way in (1, -1):
            got["sa", 0, way, part].wait_recv()
        full = total(ta_ref[z, part], rap_ref[0, part], ram_ref[0, part])
        saf_ref[part] = full
        sa_ref[part] = full.astype(BF16)
        for k in (2, 1, 3):
            got["sax", part, k] = wire.send(sa_ref.at[part, xs(k)], rax_ref.at[part, k - 1], at_x(k))

    def sum_a_y():
        for part in range(2):
            full = saf_ref[part, x]
            for k in (1, 3, 2):
                got["sax", part, k].wait_recv()
                full = full + rax_ref[part, k - 1].astype(F32)
            saf_ref[part, x] = full
            say_ref[part] = full.astype(BF16)
        got["say"] = wire.send(say_ref.at[1 - yl], ray_ref, pair)

    def sum_a_end():
        got["say"].wait_recv()
        wg_ref[:, :BLOCK] = total(saf_ref[yl, x], ray_ref[...])

    def sum_c_y(k):
        got["scy", k] = wire.send(tc_ref.at[zs(k), 1 - yl], rcy_ref.at[k], pair)

    def sum_c_hop(k, way):
        come = rcp_ref if way == 1 else rcm_ref
        rel = k if way == 1 else 8 - k
        got["scy", rel].wait_recv()
        parts = [tc_ref[zs(rel), yl], rcy_ref[rel]]
        if ("sc", k, way) in got:
            got["sc", k, way].wait_recv()
            parts.append(come[k])
        tc_ref[zs(rel), yl] = total(*parts).astype(BF16)
        got["sc", k - 1, way] = wire.send(tc_ref.at[zs(rel), yl], come.at[k - 1], z_next(way))

    def sum_c_step(k):
        for way in (1, -1):
            sum_c_hop(k, way)

    def sum_c_x():
        got["scy", 0].wait_recv()
        for way in (1, -1):
            got["sc", 0, way].wait_recv()
        full = total(tc_ref[z, yl], rcy_ref[0], rcp_ref[0], rcm_ref[0])
        scf_ref[...] = full
        sc_ref[...] = full.astype(BF16)
        for k in (2, 1, 3):
            got["scx", k] = wire.send(sc_ref.at[xs(k)], rcx_ref.at[k - 1], at_x(k))

    def sum_c_end():
        full = scf_ref[x]
        for k in (1, 3, 2):
            got["scx", k].wait_recv()
            full = full + rcx_ref[k - 1].astype(F32)
        wg_ref[:, BLOCK:HALF] = full

    def sum_b_first(k, side):
        other = 4 - side
        come = rbp_ref if side == 1 else rbm_ref
        back = rbm_ref if side == 1 else rbp_ref
        got["sb2", k] = wire.send(tb_ref.at[zs(k), :, xs(2)], come.at[k, 1], at_x(side))
        got["sb1", k, other] = wire.send(tb_ref.at[zs(k), :, xs(other)], back.at[k, 0], at_x(other))

    def sum_b_second(k, side):
        come = rbp_ref if side == 1 else rbm_ref
        got["sb2", k].wait_recv()
        at = (zs(k), slice(None), xs(side))
        tb_ref[at] = total(tb_ref[at], come[k, 1]).astype(BF16)
        got["sb1", k, side] = wire.send(tb_ref.at[at], come.at[k, 0], at_x(side))

    def sum_b_y(k):
        for side in (1, 3):
            got["sb1", k, side].wait_recv()
        full = total(tb_ref[zs(k), :, x], rbp_ref[k, 0], rbm_ref[k, 0])
        sbf_ref[k] = full
        sby_ref[k] = full.astype(BF16)
        got["sby", k] = wire.send(sby_ref.at[k, 1 - yl], rby_ref.at[k], pair)

    def sum_b_z(k):
        got["sby", k].wait_recv()
        full = total(sbf_ref[k, yl], rby_ref[k])
        if k:
            sbz_ref[k] = full.astype(BF16)
            got["sbz", k] = wire.send(sbz_ref.at[k], rbz_ref.at[k - 1], at_z(k))
        else:
            sbf_ref[0, 0] = full

    def sum_b_end():
        full = sbf_ref[0, 0]
        for k in range(1, 8):
            got["sbz", k].wait_recv()
            full = full + rbz_ref[k - 1].astype(F32)
        wg_ref[:, HALF:] = full

    def table_z():
        here = lax.dot_general(
            gb_ref[...], oh_ref[...], (((1,), (1,)), ((), ())),
            precision=lax.Precision.HIGHEST, preferred_element_type=F32,
        )
        tz_ref[...] = jnp.concatenate([here, jnp.zeros((HEADS, BLOCK - 32), F32)], axis=1)
        for k in range(1, 8):
            got["tz", k] = wire.send(tz_ref, rtz_ref.at[k - 1], at_z(k))

    def table_xy():
        full = tz_ref[...]
        for k in range(1, 8):
            got["tz", k].wait_recv()
            full = full + rtz_ref[k - 1]
        tx_ref[...] = full
        for k, device in enumerate(around):
            got["tx", k] = wire.send(tx_ref, rtx_ref.at[k], device)

    def table_end():
        full = tx_ref[...]
        for k in range(7):
            got["tx", k].wait_recv()
            full = full + rtx_ref[k]
        tg_ref[...] = full[:, :32]

    def sums_start(i):
        k = KS[i]
        term(k)
        if k == 4:
            sum_a_hop(4, 1, 0)
            sum_a_hop(4, -1, 1)
        if k == 3:
            sum_a_hop(3, 1, 1)
        if k == 5:
            sum_a_hop(3, -1, 0)
        sum_c_y(k)
        sum_b_first(k, 1 if i % 2 == 0 else 3)

    prepare()
    gather_first()
    up_hand_on(0)
    softmax_head(0)
    up_hand_on(1)
    gather_b_step(1)
    gather_a_start()
    up_hand_on(2)
    softmax_head(1)
    gather_b_across(0)
    up_share(0)
    gather_b_step(2)

    up_end(0)
    up_hand_on(3)
    up_share(1)
    sums_start(0)
    gather_b_across(1)
    gather_b_across(7)
    softmax_head(2)
    up_end(1)
    up_hand_on(4)
    up_share(2)
    sums_start(1)
    gather_a_step(1)
    softmax_head(3)
    up_end(2)
    up_hand_on(5)
    up_share(3)
    sums_start(2)
    gather_b_step(3)
    gather_b_across(2)
    gather_b_across(6)
    softmax_head(4)
    up_end(3)
    up_hand_on(6)
    up_share(4)
    sums_start(3)
    sum_a_hop(3, 1, 0)
    sum_a_hop(3, -1, 1)
    sum_c_hop(4, 1)
    gather_a_step(2)
    softmax_head(5)
    up_end(4)
    up_hand_on(7)
    up_share(5)
    sums_start(4)
    gather_b_step(4)
    gather_b_across(3)
    gather_b_across(5)
    sum_b_second(4, 1)
    sum_b_second(3, 3)
    softmax_head(6)
    up_end(5)
    up_share(6)
    sums_start(5)
    sum_a_step(2)
    sum_c_step(3)
    gather_a_step(3)
    softmax_head(7)
    up_end(6)
    up_share(7)
    sums_start(6)
    gather_b_across(4)
    sum_b_second(5, 1)
    sum_b_second(2, 3)
    sum_b_y(4)
    sum_b_y(3)
    up_end(7)
    sums_start(7)
    sum_a_step(1)
    sum_c_step(2)
    gather_a_end()
    context(0, 0)
    context(0, 1)
    gather_b_end()
    sum_b_second(6, 1)
    sum_b_second(1, 3)
    context(1, 0)
    context(1, 1)
    backward_head(0)
    sum_b_second(7, 1)
    sum_b_second(0, 3)
    sum_b_y(5)
    sum_b_y(2)
    backward_head(1)
    sum_c_step(1)
    sum_b_z(4)
    sum_b_z(3)
    backward_head(2)
    sum_b_y(6)
    sum_b_y(1)
    backward_head(3)
    sum_a_x(0)
    sum_a_x(1)
    sum_b_y(7)
    sum_b_y(0)
    backward_head(4)
    sum_b_z(5)
    sum_b_z(2)
    sum_c_x()
    backward_head(5)
    sum_b_z(6)
    sum_b_z(1)
    backward_head(6)
    sum_a_y()
    sum_b_z(7)
    sum_b_z(0)
    backward_head(7)
    table_z()
    sum_c_end()
    sum_a_end()
    table_xy()
    sum_b_end()
    table_end()
    wire.finish()


def carry(*refs):
    for src, dst in zip(refs[:5], refs[5:]):
        dst[...] = src[...]


def on_device(queries, keys, values, attended, upstream, out_weight, bias_table, buckets, segments):
    anywhere = pl.BlockSpec(memory_space=pl.ANY)
    inside = pl.BlockSpec(memory_space=pltpu.VMEM)
    bf, f4 = (lambda *s: pltpu.VMEM(s, BF16)), (lambda *s: pltpu.VMEM(s, F32))
    shapes = (
        jax.ShapeDtypeStruct((ROWS, FEAT), BF16),
        jax.ShapeDtypeStruct((ROWS, FEAT), BF16),
        jax.ShapeDtypeStruct((ROWS, FEAT), BF16),
        jax.ShapeDtypeStruct((64, FEAT), F32),
        jax.ShapeDtypeStruct((HEADS, 32), F32),
    )
    made = pl.pallas_call(
        kernel,
        out_shape=shapes,
        in_specs=[anywhere] * 6 + [inside] * 3,
        out_specs=(inside,) * 5,
        scratch_shapes=[
            bf(ROWS, FEAT), bf(ROWS, FEAT), bf(ROWS, FEAT), bf(ROWS, FEAT),
            bf(ROWS, D), bf(ROWS, FEAT),
            bf(8, 2, 4, 64, HALF), bf(8, 2, 4, 64, HALF),
            bf(8, 64, FEAT), bf(8, 64, FEAT),
            bf(8, 2, 4, 64, BLOCK), bf(8, 2, 4, 64, BLOCK), bf(8, 2, 4, 64, HALF),
            bf(4, 2, 4, 64, BLOCK), bf(4, 2, 4, 64, BLOCK), bf(2, 4, 64, BLOCK), f4(2, 4, 64, BLOCK),
            bf(2, 3, 64, BLOCK), bf(64, BLOCK), bf(2, 64, BLOCK),
            bf(8, 4, 64, BLOCK), bf(4, 4, 64, BLOCK), bf(4, 4, 64, BLOCK), bf(4, 64, BLOCK),
            f4(4, 64, BLOCK), bf(3, 64, BLOCK),
            bf(8, 2, 2, 64, HALF), bf(8, 2, 2, 64, HALF), bf(8, 2, 64, HALF), f4(8, 2, 64, HALF),
            bf(8, 64, HALF), bf(8, 64, HALF), bf(7, 64, HALF),
            f4(HEADS, ROWS, ROWS), f4(HEADS, ROWS), f4(ROWS, ROWS), bf(ROWS, ROWS), bf(ROWS, ROWS),
            f4(5, BLOCK, BLOCK), f4(HEADS, WIDE), f4(32, WIDE), f4(HEADS, WIDE), f4(8, WIDE),
            bf(ROWS, BLOCK), bf(ROWS, BLOCK), f4(BLOCK, ROWS), f4(ROWS, BLOCK), f4(ROWS, BLOCK),
            f4(HEADS, BLOCK), f4(7, HEADS, BLOCK), f4(HEADS, BLOCK), f4(7, HEADS, BLOCK),
            pltpu.SemaphoreType.DMA((7,)),
            pltpu.SemaphoreType.DMA((N_SEM,)),
            pltpu.SemaphoreType.DMA((N_SEM,)),
        ],
        compiler_params=pltpu.CompilerParams(
            collective_id=0, has_side_effects=True, vmem_limit_bytes=60 * 1024 * 1024
        ),
    )(
        queries, keys, values, attended, upstream, out_weight.T, bias_table.T, buckets[None, :], segments[None, :]
    )
    dq, dk, dv, wg, tg = pl.pallas_call(
        carry,
        out_shape=shapes,
        in_specs=[inside] * 5,
        out_specs=(inside,) * 5,
    )(*made)
    return dq, dk, dv, wg, tg.T


def solution(mesh):
    in_specs = (
        P("dp", "tensor"),
        P("dp", "tensor"),
        P("dp", "tensor"),
        P("dp", "tensor"),
        P(("dp", "tensor"), None),
        P("tensor", "dp"),
        P(None, "tensor"),
        P(),
        P("dp"),
    )
    out_specs = (
        P("dp", "tensor"),
        P("dp", "tensor"),
        P("dp", "tensor"),
        P("dp", "tensor"),
        P(None, "tensor"),
    )
    return jax.shard_map(
        on_device, mesh=mesh, in_specs=in_specs, out_specs=out_specs, check_vma=False
    )
```
